32 devices in a mesh: dp: 2 (over x), ctx: 8 (over z, y), head: 2 (over core).
Axes of the slice: x: 2, y: 2, z: 4, core: 2. Of those that a mesh axis runs over, the one named last changes fastest.
Arguments:
- queries: bfloat16 [2, 1024, 4096], P('dp', 'ctx', 'head'), may hold values from -200 to 200
- targets: bfloat16 [2, 1024, 4096], P('dp', 'ctx', 'head'), may hold values from -3 to 3
- document_keys: bfloat16 [2, 1024, 256], P('dp', 'ctx', 'head'), may hold values from -6 to 6
- document_values: bfloat16 [2, 1024, 256], P('dp', 'ctx', 'head'), may hold values from -6 to 6
- doc_pos: int32 [2, 1024], P('dp', 'ctx'), may hold values from 0 to 1023, each once within a row
- cart_keys: bfloat16 [128, 256], P('ctx', 'head'), may hold values from -8 to 8
- cartridge_values: bfloat16 [128, 256], P('ctx', 'head'), may hold values from -6 to 6
- master: float32 [128, 2, 256], P('ctx', 'head', 'dp'), may hold values from -5 to 5
- first_moment1: float32 [128, 2, 256], P('ctx', 'head', 'dp'), may hold values from -4 to 4
- second_moment2: float32 [128, 2, 256], P('ctx', 'head', 'dp'), may hold values from 0.1 to 2
Outputs:
- new_out: bfloat16 [2, 1024, 4096], P('dp', 'ctx', 'head')
- new_master: float32 [128, 2, 256], P('ctx', 'head', 'dp')
- new_moment1: float32 [128, 2, 256], P('ctx', 'head', 'dp')
- new_moment2: float32 [128, 2, 256], P('ctx', 'head', 'dp')
The draws below stay inside these ranges and needn't reach their ends.
Inputs may be any that keep to these rules, and one draw needn't show every extreme that they name: Each row of doc_pos holds every position of the document once.
All inputs are finite; a program needn't handle non-finite values.
Results may differ from the reference program's by a relative error of at most 0.015.
Values may be sent and summed in bfloat16 or wider, within the bound.
No kernel may reach another device: no remote copies, remote signals or barrier semaphores. Data moves between devices by JAX's collectives and lax.ppermute only.
A program may use at most 64 MiB of HBM per device.

```python
import math
import jax
import jax.numpy as jnp
from jax import lax

HEAD_SIZE = 128
HQ = 32
KEY_VALUE_HEADS = 2
GROUP = 16
DOCUMENT_LEN = 1024
CARTRIDGE_LEN = 128
N_DP = 2


def starting_keys(key):
    unscaled_input = jax.random.normal(jax.random.fold_in(key, 101), (CARTRIDGE_LEN, KEY_VALUE_HEADS, HEAD_SIZE), jnp.float32)
    unscaled_input = jnp.clip(unscaled_input, -5.0, 5.0)
    return unscaled_input


def draw_cart_keys(key, part):
    return starting_keys(key).reshape(CARTRIDGE_LEN, KEY_VALUE_HEADS * HEAD_SIZE).astype(jnp.bfloat16)


def draw_queries(key, part):
    drawn = jnp.clip(jax.random.normal(jax.random.fold_in(key, 202), (N_DP, DOCUMENT_LEN, HQ, HEAD_SIZE), jnp.float32), -5.0, 5.0)
    return drawn.reshape(N_DP, DOCUMENT_LEN, HQ * HEAD_SIZE).astype(jnp.bfloat16)


def block_scale(rng, shape, split, low, high):
    def one(position, parts):
        draws = jax.random.uniform(jax.random.fold_in(jax.random.fold_in(rng, 6), position), (parts,), jnp.float32, low / len(split), high / len(split))
        return jnp.repeat(jnp.exp(draws), shape[position] // parts).reshape((-1,) + (1,) * (len(shape) - position - 1))

    gain = one(*split[0])
    for cut in split[1:]:
        gain = gain * one(*cut)
    return gain


def noise(own_key, extent, deviation, limit, shards=(), kind=jnp.bfloat16):
    result = deviation * jax.random.normal(own_key, extent, jnp.float32)
    if shards:
        result = result * block_scale(own_key, extent, shards, -0.22, 0.18)
    return jnp.clip(result, -limit, limit).astype(kind)


def setup_inputs(seed: int = 0) -> dict:
    splits = jax.random.split(jax.random.key(seed), 11)
    return {
        "queries": draw_queries(jax.random.fold_in(splits[10], 71), 0),
        "targets": noise(splits[1], (N_DP, DOCUMENT_LEN, HQ * HEAD_SIZE), 0.5, 3.0, ((0, 2), (1, 8), (2, 2))),
        "document_keys": noise(splits[2], (N_DP, DOCUMENT_LEN, KEY_VALUE_HEADS * HEAD_SIZE), 1.0, 6.0, ((0, 2), (1, 8), (2, 2))),
        "document_values": noise(splits[3], (N_DP, DOCUMENT_LEN, KEY_VALUE_HEADS * HEAD_SIZE), 1.0, 6.0, ((0, 2), (1, 8), (2, 2))),
        "doc_pos": jax.vmap(lambda own: jax.random.permutation(own, DOCUMENT_LEN))(jax.random.split(splits[4], N_DP)).reshape((N_DP, DOCUMENT_LEN)).astype(jnp.int32),
        "cart_keys": draw_cart_keys(jax.random.fold_in(splits[10], 71), 0),
        "cartridge_values": noise(splits[6], (CARTRIDGE_LEN, KEY_VALUE_HEADS * HEAD_SIZE), 1.0, 6.0, ((0, 8), (1, 2))),
        "master": noise(splits[7], (CARTRIDGE_LEN, KEY_VALUE_HEADS, 2 * HEAD_SIZE), 1.0, 5.0, ((0, 8), (1, 2), (2, 2)), jnp.float32),
        "first_moment1": noise(splits[8], (CARTRIDGE_LEN, KEY_VALUE_HEADS, 2 * HEAD_SIZE), 1.0, 4.0, ((0, 8), (1, 2), (2, 2)), jnp.float32),
        "second_moment2": jnp.clip(jnp.exp(math.log(2.0) - 2.9957323 * jax.random.uniform(splits[9], (CARTRIDGE_LEN, KEY_VALUE_HEADS, 2 * HEAD_SIZE), jnp.float32) ** block_scale(splits[9], (CARTRIDGE_LEN, KEY_VALUE_HEADS, 2 * HEAD_SIZE), ((0, 8), (1, 2), (2, 2)), -0.2, 0.2)), 0.1, 2.0),
    }


neg_big = -1e+30

def scores_of(left, right):
    return lax.dot_general(left, right, (((1,), (1,)), ((), ())), preferred_element_type=jnp.float32)

def attend(flat_q, query_pos, keys_c, values_c, keys_d, values_d, key_pos):
    scale = HEAD_SIZE ** (-0.5)
    cart_s = scores_of(flat_q, keys_c) * scale
    doc_s = scores_of(flat_q, keys_d) * scale
    allowed = key_pos[None, :] <= query_pos[:, None]
    doc_s = jnp.where(allowed, doc_s, neg_big)
    top = jnp.maximum(lax.optimization_barrier(jnp.max(cart_s, axis=1)), lax.optimization_barrier(jnp.max(doc_s, axis=1)))
    weight_c = jnp.exp(cart_s - top[:, None])
    weight_d = jnp.where(allowed, jnp.exp(doc_s - top[:, None]), 0.0)
    total = lax.optimization_barrier(jnp.sum(weight_c, axis=1)) + lax.optimization_barrier(jnp.sum(weight_d, axis=1))
    accum = jnp.dot(weight_c.astype(jnp.bfloat16), values_c, preferred_element_type=jnp.float32)
    accum = accum + jnp.dot(weight_d.astype(jnp.bfloat16), values_d, preferred_element_type=jnp.float32)
    return (top, total, accum / total[:, None], cart_s)

def reference(queries, targets, document_keys, document_values, doc_pos, cart_keys, cartridge_values, master, first_moment1, second_moment2):
    block = math.gcd(DOCUMENT_LEN, 512)
    nblock = DOCUMENT_LEN // block
    scale = HEAD_SIZE ** (-0.5)
    steps_all = jnp.arange(N_DP * nblock, dtype=jnp.int32)

    def inputs(index, group_index):
        batch = (index // nblock).astype(jnp.int32)
        first = (index % nblock * block).astype(jnp.int32)
        col = jnp.int32(group_index * GROUP * HEAD_SIZE)
        flat_q = lax.dynamic_slice(queries, (batch, first, col), (1, block, GROUP * HEAD_SIZE))[0].reshape(block * GROUP, HEAD_SIZE)
        flat_t = lax.dynamic_slice(targets, (batch, first, col), (1, block, GROUP * HEAD_SIZE))[0].reshape(block * GROUP, HEAD_SIZE)
        kcol = jnp.int32(group_index * HEAD_SIZE)
        keys_d = lax.dynamic_slice(document_keys, (batch, jnp.int32(0), kcol), (1, DOCUMENT_LEN, HEAD_SIZE))[0]
        values_d = lax.dynamic_slice(document_values, (batch, jnp.int32(0), kcol), (1, DOCUMENT_LEN, HEAD_SIZE))[0]
        key_pos = lax.dynamic_slice(doc_pos, (batch, jnp.int32(0)), (1, DOCUMENT_LEN))[0]
        query_pos = jnp.repeat(lax.dynamic_slice_in_dim(key_pos, first, block), GROUP)
        return (flat_q, flat_t, keys_d, values_d, key_pos, query_pos)
    grads = []
    for group_index in range(KEY_VALUE_HEADS):
        keys_c = cart_keys[:, group_index * HEAD_SIZE:(group_index + 1) * HEAD_SIZE]
        values_c = cartridge_values[:, group_index * HEAD_SIZE:(group_index + 1) * HEAD_SIZE]

        def step(carry, index):
            flat_q, flat_t, keys_d, values_d, key_pos, query_pos = inputs(index, group_index)
            top, total, out, cart_s = attend(flat_q, query_pos, keys_c, values_c, keys_d, values_d, key_pos)
            d_out = out - flat_t.astype(jnp.float32)
            delta = lax.optimization_barrier(jnp.sum(d_out * out, axis=1))
            d_out_b = d_out.astype(jnp.bfloat16)
            probs = jnp.exp(cart_s - top[:, None]) / total[:, None]
            d_probs = scores_of(d_out_b, values_c)
            d_scores = probs * (d_probs - delta[:, None])
            grad_k = lax.dot_general(d_scores.astype(jnp.bfloat16), flat_q, (((0,), (0,)), ((), ())), preferred_element_type=jnp.float32) * scale
            grad_v = lax.dot_general(probs.astype(jnp.bfloat16), d_out_b, (((0,), (0,)), ((), ())), preferred_element_type=jnp.float32)
            return (carry + jnp.concatenate([grad_k, grad_v], axis=1), None)
        summed, _ = lax.scan(step, jnp.zeros((CARTRIDGE_LEN, 2 * HEAD_SIZE), jnp.float32), steps_all)
        grads.append(summed)
    grad_all = jnp.stack(grads, axis=1)
    rms = jnp.sqrt(jnp.mean(grad_all * grad_all) + 1e-06)
    normed = grad_all / rms
    new_moment1 = 0.8 * first_moment1 + 0.2 * normed
    new_moment2 = 0.95 * second_moment2 + 0.05 * normed * normed
    new_master = master - 0.1 * new_moment1 / (jnp.sqrt(new_moment2) + 1e-08)
    copies = new_master.astype(jnp.bfloat16)
    outs = []
    for group_index in range(KEY_VALUE_HEADS):
        keys_c = copies[:, group_index, :HEAD_SIZE]
        values_c = copies[:, group_index, HEAD_SIZE:]

        def again(index):
            flat_q, flat_t, keys_d, values_d, key_pos, query_pos = inputs(index, group_index)
            top, total, out, cart_s = attend(flat_q, query_pos, keys_c, values_c, keys_d, values_d, key_pos)
            return out.astype(jnp.bfloat16)
        outs.append(lax.map(again, steps_all).reshape(N_DP, nblock, block, GROUP, HEAD_SIZE))
    stacked = jnp.stack(outs, axis=0)
    new_out = jnp.transpose(stacked, (1, 2, 3, 0, 4, 5)).reshape(N_DP, DOCUMENT_LEN, HQ * HEAD_SIZE)
    return (new_out, new_master, new_moment1, new_moment2)
```

```python
import functools
import math

import jax
import jax.numpy as jnp
from jax import lax
from jax.experimental import pallas as pl
from jax.experimental.pallas import tpu as pltpu
from jax.sharding import PartitionSpec as P


beta_one = 0.8
beta_two = 0.95
learn_rate = 0.1
adam_eps = 1e-08
norm_eps = 1e-06
neg_big = -1e30
log2_e = math.log2(math.e)
pos_base = 256.0
f32, bf16 = jnp.float32, jnp.bfloat16


def xor_steps(size):
    assert size & (size - 1) == 0
    return [1 << b for b in reversed(range(size.bit_length() - 1))]


def swap(x, axis, mask, size):
    return lax.ppermute(x, axis, [(i, i ^ mask) for i in range(size)])


def place(mask, steps):
    at = 0
    for n, step in enumerate(steps):
        bit = step.bit_length() - 1
        at = at + (((mask >> bit) & 1) << n)
    return at


def nt(a, b):
    return lax.dot_general(a, b, (((1,), (1,)), ((), ())), preferred_element_type=f32)


def tn(a, b):
    return lax.dot_general(a, b, (((0,), (0,)), ((), ())), preferred_element_type=f32)


def nn(a, b):
    return jnp.dot(a, b, preferred_element_type=f32)


def pack_kernel(k, v, pos, ck, cv, ma, m1, m2, msg, st):
    rows, crows, hd = k.shape[1], ck.shape[0], k.shape[2]
    msg[0:rows] = k[0]
    msg[rows : 2 * rows] = v[0]
    at = 2 * rows
    msg[at : at + crows] = ck[...]
    msg[at + crows : at + 2 * crows] = cv[...]
    at += 2 * crows
    p = pos[...].astype(f32)
    hi = jnp.floor(p * (1.0 / pos_base))
    lo = p - hi * pos_base
    line = lax.broadcasted_iota(jnp.int32, (16, hd), 0)
    both = jnp.where(line == 0, jnp.broadcast_to(hi, (16, hd)), jnp.broadcast_to(lo, (16, hd)))
    msg[at : at + 16] = both.astype(bf16)
    for n, ref in enumerate((ma, m1, m2)):
        st[n * crows : (n + 1) * crows] = ref[:, 0, :]


def attention_kernel(steps, scale, per, q, t, msgs, acc_out, top_out, grad):
    rows = q.shape[0]
    hd = msgs.shape[1]
    group = q.shape[1] // hd
    size = 1 << len(steps)
    stride = msgs.shape[0] // size
    crows = (stride - 2 * rows - 16) // 2
    me = lax.axis_index("ctx")
    two = scale * log2_e

    def position(j):
        at = j * stride + 2 * rows + 2 * crows
        two_rows = msgs[at : at + 16].astype(f32)
        return two_rows[0:1] * pos_base + two_rows[1:2]

    query_pos = jnp.broadcast_to(position(0), (rows, rows)).T
    key_pos = jnp.concatenate([position(j) for j in range(size)], axis=1)
    reach = jnp.concatenate([query_pos] * size, axis=1) if size > 1 else query_pos
    bias = jnp.where(jnp.broadcast_to(key_pos, reach.shape) <= reach, 0.0, neg_big)
    keys = jnp.concatenate([msgs[j * stride : j * stride + rows] for j in range(size)], axis=0)
    values = jnp.concatenate([msgs[j * stride + rows : j * stride + 2 * rows] for j in range(size)], axis=0)
    values = jnp.concatenate([values, jnp.ones_like(values)], axis=1)
    ck_list, cv_list = [], []
    for g in range(size):
        at = place(me ^ g, steps) * stride + 2 * rows
        ck_list.append(msgs[pl.ds(pl.multiple_of(at, 16), crows)])
        cv_list.append(msgs[pl.ds(pl.multiple_of(at + crows, 16), crows)])
    cart_k = jnp.concatenate(ck_list, axis=0)
    cart_v = jnp.concatenate(cv_list, axis=0)
    cart_vx = jnp.concatenate([cart_v, jnp.ones_like(cart_v)], axis=1)
    span = per * rows
    gk = jnp.zeros((cart_k.shape[0], hd), f32)
    gv = jnp.zeros((cart_k.shape[0], hd), f32)
    for b in range(group // per):
        heads = range(b * per, (b + 1) * per)
        qh = jnp.concatenate([q[:, h * hd : (h + 1) * hd] for h in heads], axis=0)
        s = nt(qh, keys) * two
        s = (s.reshape(per, rows, s.shape[1]) + bias[None]).reshape(s.shape)
        top = jnp.max(s, axis=1, keepdims=True)
        w = jnp.exp2(s - top).astype(bf16)
        acc = nn(w, values)
        acc_out[b * span : (b + 1) * span] = acc
        top_out[b * span : (b + 1) * span] = jnp.broadcast_to(top, (span, hd))
        sc = nt(qh, cart_k) * two
        both = jnp.maximum(top, jnp.max(sc, axis=1, keepdims=True))
        wc = jnp.exp2(sc - both)
        full = acc * jnp.exp2(top - both) + nn(wc.astype(bf16), cart_vx)
        inv = 1.0 / full[:, hd:]
        out = full[:, :hd] * inv
        goal = jnp.concatenate([t[:, h * hd : (h + 1) * hd] for h in heads], axis=0)
        d_out = out - goal.astype(f32)
        delta = jnp.sum(d_out * out, axis=1, keepdims=True)
        d_out_b = d_out.astype(bf16)
        probs = wc * inv[:, 0:1]
        ds = probs * (nt(d_out_b, cart_v) - delta)
        gk = gk + tn(ds.astype(bf16), qh)
        gv = gv + tn(probs.astype(bf16), d_out_b)
    grad[:, :hd] = (gk * scale).astype(bf16)
    grad[:, hd:] = gv.astype(bf16)


def square_kernel(a, b, total, squares):
    g = a[...].astype(f32) + b[...].astype(f32)
    total[...] = g
    squares[...] = jnp.broadcast_to(jnp.sum(g * g, keepdims=True), squares.shape)


def update(g, ma, m1, m2):
    one = beta_one * m1 + (1.0 - beta_one) * g
    two = beta_two * m2 + (1.0 - beta_two) * g * g
    return one, two, ma - learn_rate * one / (jnp.sqrt(two) + adam_eps)


def final_kernel(steps, dp_steps, scale, per, count, q, acc_in, top_in, g, sq_a, sq_b, st, ma, m1, m2, out, ma_o, m1_o, m2_o, cart):
    rows, hd = q.shape[0], acc_in.shape[1] // 2
    group = q.shape[1] // hd
    size, n_dp = 1 << len(steps), 1 << len(dp_steps)
    crows, width = ma.shape[0], ma.shape[2]
    me, my_dp = lax.axis_index("ctx"), lax.axis_index("dp")
    two = scale * log2_e
    mean = (sq_a[0:1, 0:1] + sq_b[0:1, 0:1]) * (1.0 / count)
    inv_rms = 1.0 / jnp.sqrt(mean + norm_eps)
    mine = g[pl.ds(pl.multiple_of(me * crows, crows), crows)]
    own = mine[:, 0:width]
    for d in range(1, n_dp):
        own = jnp.where(my_dp == d, mine[:, d * width : (d + 1) * width], own)
    one, sec, new = update(own * inv_rms, ma[:, 0, :], m1[:, 0, :], m2[:, 0, :])
    m1_o[:, 0, :] = one
    m2_o[:, 0, :] = sec
    ma_o[:, 0, :] = new
    for r in range(size):
        parts = [[], [], []]
        for d in range(n_dp):
            at = (place(me ^ r, steps) * n_dp + place(my_dp ^ d, dp_steps)) * 3 * crows
            for n in range(3):
                parts[n].append(st[pl.ds(pl.multiple_of(at + n * crows, crows), crows)])
        ma_r, m1_r, m2_r = (jnp.concatenate(x, axis=1) for x in parts)
        _, _, new = update(g[r * crows : (r + 1) * crows] * inv_rms, ma_r, m1_r, m2_r)
        cart[r * crows : (r + 1) * crows] = new.astype(bf16)
    cart_k = cart[:, :hd]
    cart_v = cart[:, hd:]
    cart_vx = jnp.concatenate([cart_v, jnp.ones_like(cart_v)], axis=1)
    span = per * rows
    for b in range(group // per):
        heads = range(b * per, (b + 1) * per)
        qh = jnp.concatenate([q[:, h * hd : (h + 1) * hd] for h in heads], axis=0)
        acc = acc_in[b * span : (b + 1) * span]
        top = top_in[b * span : (b + 1) * span][:, 0:1]
        sc = nt(qh, cart_k) * two
        both = jnp.maximum(top, jnp.max(sc, axis=1, keepdims=True))
        wc = jnp.exp2(sc - both).astype(bf16)
        full = acc * jnp.exp2(top - both) + nn(wc, cart_vx)
        res = (full[:, :hd] / full[:, hd:]).astype(bf16)
        for n, h in enumerate(heads):
            out[:, h * hd : (h + 1) * hd] = res[n * rows : (n + 1) * rows]


VMEM = pl.BlockSpec(memory_space=pltpu.VMEM)


def call(body, outs, n_in, scratch=(), limit=40):
    return pl.pallas_call(
        body,
        out_shape=outs,
        in_specs=[VMEM] * n_in,
        out_specs=tuple(VMEM for _ in outs),
        scratch_shapes=list(scratch),
        compiler_params=pltpu.CompilerParams(vmem_limit_bytes=limit * 2**20),
    )


def local(sizes, queries, targets, document_keys, document_values, doc_pos, cart_keys, cartridge_values, master, first_moment1, second_moment2):
    n_dp, n_ctx, n_head = sizes
    hd = document_keys.shape[2]
    rows = queries.shape[1]
    group = queries.shape[2] // hd
    crows = cart_keys.shape[0]
    scale = hd ** (-0.5)
    per = math.gcd(group, 4)
    steps, dp_steps, head_steps = xor_steps(n_ctx), xor_steps(n_dp), xor_steps(n_head)
    sds = jax.ShapeDtypeStruct
    msg, st = call(
        pack_kernel,
        (sds((2 * rows + 2 * crows + 16, hd), bf16), sds((3 * crows, master.shape[2]), f32)),
        8,
    )(document_keys, document_values, doc_pos, cart_keys, cartridge_values, master, first_moment1, second_moment2)
    for s in steps:
        msg = jnp.concatenate([msg, swap(msg, "ctx", s, n_ctx)], axis=0)
    for s in dp_steps:
        st = jnp.concatenate([st, swap(st, "dp", s, n_dp)], axis=0)
    for s in steps:
        st = jnp.concatenate([st, swap(st, "ctx", s, n_ctx)], axis=0)
    q, t = queries[0], targets[0]
    cart = n_ctx * crows
    acc, top, grad = call(
        functools.partial(attention_kernel, steps, scale, per),
        (sds((rows * group, 2 * hd), f32), sds((rows * group, hd), f32), sds((cart, 2 * hd), bf16)),
        3,
    )(q, t, msg)
    chain = [("dp", s, n_dp) for s in dp_steps] + [("ctx", s, n_ctx) for s in steps]
    for n, (axis, s, size) in enumerate(chain):
        other = swap(grad, axis, s, size)
        if n + 1 < len(chain):
            grad = (grad.astype(f32) + other.astype(f32)).astype(bf16)
    total, squares = call(square_kernel, (sds((cart, 2 * hd), f32), sds((8, hd), f32)), 2)(grad, other)
    mine = squares
    theirs = jnp.zeros_like(squares)
    for n, s in enumerate(head_steps):
        if n:
            mine = mine + theirs
        theirs = swap(mine, "head", s, n_head)
    count = master.size * n_dp * n_ctx * n_head
    new_out, new_master, new_m1, new_m2 = call(
        functools.partial(final_kernel, steps, dp_steps, scale, per, count),
        (sds((rows, group * hd), bf16), sds(master.shape, f32), sds(master.shape, f32), sds(master.shape, f32)),
        10,
        [pltpu.VMEM((cart, 2 * hd), bf16)],
    )(q, acc, top, total, mine, theirs, st, master, first_moment1, second_moment2)
    return (new_out[None], new_master, new_m1, new_m2)


def solution(mesh):
    in_specs = (
        P("dp", "ctx", "head"),
        P("dp", "ctx", "head"),
        P("dp", "ctx", "head"),
        P("dp", "ctx", "head"),
        P("dp", "ctx"),
        P("ctx", "head"),
        P("ctx", "head"),
        P("ctx", "head", "dp"),
        P("ctx", "head", "dp"),
        P("ctx", "head", "dp"),
    )
    out_specs = (
        P("dp", "ctx", "head"),
        P("ctx", "head", "dp"),
        P("ctx", "head", "dp"),
        P("ctx", "head", "dp"),
    )
    sizes = (mesh.shape["dp"], mesh.shape["ctx"], mesh.shape["head"])
    return jax.shard_map(
        functools.partial(local, sizes), mesh=mesh, in_specs=in_specs, out_specs=out_specs, check_vma=False
    )
```

```python
import functools
import math

import jax
import jax.numpy as jnp
from jax import lax
from jax.experimental import pallas as pl
from jax.experimental.pallas import tpu as pltpu
from jax.sharding import PartitionSpec as P


beta_one = 0.8
beta_two = 0.95
learn_rate = 0.1
adam_eps = 1e-08
norm_eps = 1e-06
neg_big = -1e30
log2_e = math.log2(math.e)
pos_base = 256.0
f32, bf16 = jnp.float32, jnp.bfloat16


def xor_steps(size):
    assert size & (size - 1) == 0
    return [1 << b for b in reversed(range(size.bit_length() - 1))]


def swap(x, axis, mask, size):
    return lax.ppermute(x, axis, [(i, i ^ mask) for i in range(size)])


def place(mask, steps):
    at = 0
    for n, step in enumerate(steps):
        bit = step.bit_length() - 1
        at = at + (((mask >> bit) & 1) << n)
    return at


def nt(a, b):
    return lax.dot_general(a, b, (((1,), (1,)), ((), ())), preferred_element_type=f32)


def tn(a, b):
    return lax.dot_general(a, b, (((0,), (0,)), ((), ())), preferred_element_type=f32)


def nn(a, b):
    return jnp.dot(a, b, preferred_element_type=f32)


def pack_kernel(k, v, pos, ck, cv, ma, m1, m2, msg, st, line, sems):
    rows, crows, hd = k.shape[1], ck.shape[0], k.shape[2]
    at = 2 * rows
    copies = [
        (k.at[0], msg.at[0:rows]),
        (v.at[0], msg.at[rows:at]),
        (ck, msg.at[at : at + crows]),
        (cv, msg.at[at + crows : at + 2 * crows]),
        (pos, line),
    ]
    copies += [(ref.at[:, 0, :], st.at[n * crows : (n + 1) * crows]) for n, ref in enumerate((ma, m1, m2))]
    started = [pltpu.make_async_copy(x, y, sems.at[n]) for n, (x, y) in enumerate(copies)]
    for copy in started:
        copy.start()
    for copy in started:
        copy.wait()
    at += 2 * crows
    p = line[...].astype(f32)
    hi = jnp.floor(p * (1.0 / pos_base))
    lo = p - hi * pos_base
    row = lax.broadcasted_iota(jnp.int32, (16, hd), 0)
    both = jnp.where(row == 0, jnp.broadcast_to(hi, (16, hd)), jnp.broadcast_to(lo, (16, hd)))
    msg[at : at + 16] = both.astype(bf16)


def split(refs, stride):
    return [(ref, j * stride) for ref in refs for j in range(ref.shape[0] // stride)]


def positions(ref, at, stride):
    two_rows = ref[at + stride - 16 : at + stride].astype(f32)
    return two_rows[0:1] * pos_base + two_rows[1:2]


def document_part(own, blocks, rows, stride):
    query_pos = jnp.broadcast_to(positions(own, 0, stride), (rows, rows)).T
    bias, keys, values = [], [], []
    for ref, at in blocks:
        key_pos = jnp.broadcast_to(positions(ref, at, stride), (rows, rows))
        bias.append(jnp.where(key_pos <= query_pos, 0.0, neg_big))
        keys.append(ref[at : at + rows])
        values.append(ref[at + rows : at + 2 * rows])
    values = jnp.concatenate(values, axis=0)
    return (
        jnp.concatenate(keys, axis=0),
        jnp.concatenate([values, jnp.ones_like(values)], axis=1),
        jnp.concatenate(bias, axis=1),
    )


def heads_of(ref, b, per, hd):
    return jnp.concatenate([ref[:, h * hd : (h + 1) * hd] for h in range(b * per, (b + 1) * per)], axis=0)


def attend(qh, part, two, per, state):
    keys, values, bias = part
    s = nt(qh, keys) * two
    s = (s.reshape(per, s.shape[0] // per, s.shape[1]) + bias[None]).reshape(s.shape)
    top = jnp.max(s, axis=1, keepdims=True)
    if state is None:
        return nn(jnp.exp2(s - top).astype(bf16), values), top
    acc, old = state
    top = jnp.maximum(top, old)
    return nn(jnp.exp2(s - top).astype(bf16), values) + acc * jnp.exp2(old - top), top


def chunk_kernel(n_msgs, scale, per, rows, stride, *refs):
    q, own, msgs = refs[0], refs[1], refs[2 : 2 + n_msgs]
    acc_out, top_out = refs[-2:]
    old = refs[2 + n_msgs : -2]
    hd = own.shape[1]
    part = document_part(own, split(msgs, stride), rows, stride)
    span = per * rows
    for b in range(q.shape[1] // hd // per):
        cut = slice(b * span, (b + 1) * span)
        state = (old[0][cut], old[1][cut][:, 0:1]) if old else None
        acc, top = attend(heads_of(q, b, per, hd), part, scale * log2_e, per, state)
        acc_out[cut] = acc
        top_out[cut] = jnp.broadcast_to(top, (span, hd))


def gradient_kernel(n_last, masks, scale, per, rows, stride, *refs):
    q, t, acc_in, top_in = refs[:4]
    acc_out, top_out, grad = refs[-3:]
    msgs = refs[4:-3]
    own = msgs[0]
    hd = own.shape[1]
    crows = (stride - 2 * rows - 16) // 2
    me = lax.axis_index("ctx")
    two = scale * log2_e
    part = document_part(own, split(msgs[len(msgs) - n_last :], stride), rows, stride) if n_last else None
    every = [(ref, at + 2 * rows) for ref, at in split(msgs, stride)]
    cart_k = jnp.concatenate([ref[at : at + crows] for ref, at in every], axis=0)
    cart_v = jnp.concatenate([ref[at + crows : at + 2 * crows] for ref, at in every], axis=0)
    cart_vx = jnp.concatenate([cart_v, jnp.ones_like(cart_v)], axis=1)
    span = per * rows
    gk = jnp.zeros((cart_k.shape[0], hd), f32)
    gv = jnp.zeros((cart_k.shape[0], hd), f32)
    for b in range(q.shape[1] // hd // per):
        cut = slice(b * span, (b + 1) * span)
        qh = heads_of(q, b, per, hd)
        acc, top = acc_in[cut], top_in[cut][:, 0:1]
        if part is not None:
            acc, top = attend(qh, part, two, per, (acc, top))
        acc_out[cut] = acc
        top_out[cut] = jnp.broadcast_to(top, (span, hd))
        sc = nt(qh, cart_k) * two
        both = jnp.maximum(top, jnp.max(sc, axis=1, keepdims=True))
        wc = jnp.exp2(sc - both)
        full = acc * jnp.exp2(top - both) + nn(wc.astype(bf16), cart_vx)
        inv = 1.0 / full[:, hd:]
        out = full[:, :hd] * inv
        d_out = out - heads_of(t, b, per, hd).astype(f32)
        delta = jnp.sum(d_out * out, axis=1, keepdims=True)
        d_out_b = d_out.astype(bf16)
        probs = wc * inv[:, 0:1]
        ds = probs * (nt(d_out_b, cart_v) - delta)
        gk = gk + tn(ds.astype(bf16), qh)
        gv = gv + tn(probs.astype(bf16), d_out_b)
    whole = jnp.concatenate([gk * scale, gv], axis=1).astype(bf16)
    for j, mask in enumerate(masks):
        to = pl.multiple_of((me ^ mask) * crows, crows)
        grad[pl.ds(to, crows)] = whole[j * crows : (j + 1) * crows]


def square_kernel(a, b, total, squares):
    g = a[...].astype(f32) + b[...].astype(f32)
    total[...] = g
    squares[...] = jnp.broadcast_to(jnp.sum(g * g, keepdims=True), squares.shape)


def update(g, ma, m1, m2):
    one = beta_one * m1 + (1.0 - beta_one) * g
    two = beta_two * m2 + (1.0 - beta_two) * g * g
    return one, two, ma - learn_rate * one / (jnp.sqrt(two) + adam_eps)


def final_kernel(masks, dp_steps, scale, per, count, q, acc_in, top_in, g, sq_a, sq_b, st, ma, m1, m2, out, ma_o, m1_o, m2_o, cart):
    rows, hd = q.shape[0], acc_in.shape[1] // 2
    group = q.shape[1] // hd
    n_dp = 1 << len(dp_steps)
    crows, width = ma.shape[0], ma.shape[2]
    me, my_dp = lax.axis_index("ctx"), lax.axis_index("dp")
    two = scale * log2_e
    mean = (sq_a[0:1, 0:1] + sq_b[0:1, 0:1]) * (1.0 / count)
    inv_rms = 1.0 / jnp.sqrt(mean + norm_eps)
    mine = g[pl.ds(pl.multiple_of(me * crows, crows), crows)]
    own = mine[:, 0:width]
    for d in range(1, n_dp):
        own = jnp.where(my_dp == d, mine[:, d * width : (d + 1) * width], own)
    one, sec, new = update(own * inv_rms, ma[:, 0, :], m1[:, 0, :], m2[:, 0, :])
    m1_o[:, 0, :] = one
    m2_o[:, 0, :] = sec
    ma_o[:, 0, :] = new
    for r, mask in enumerate(masks):
        parts = [[], [], []]
        for d in range(n_dp):
            at = (r * n_dp + place(my_dp ^ d, dp_steps)) * 3 * crows
            for n in range(3):
                parts[n].append(st[pl.ds(pl.multiple_of(at + n * crows, crows), crows)])
        ma_r, m1_r, m2_r = (jnp.concatenate(x, axis=1) for x in parts)
        rows_g = g[pl.ds(pl.multiple_of((me ^ mask) * crows, crows), crows)]
        _, _, new = update(rows_g * inv_rms, ma_r, m1_r, m2_r)
        cart[r * crows : (r + 1) * crows] = new.astype(bf16)
    cart_k = cart[:, :hd]
    cart_v = cart[:, hd:]
    cart_vx = jnp.concatenate([cart_v, jnp.ones_like(cart_v)], axis=1)
    span = per * rows
    for b in range(group // per):
        heads = range(b * per, (b + 1) * per)
        qh = jnp.concatenate([q[:, h * hd : (h + 1) * hd] for h in heads], axis=0)
        acc = acc_in[b * span : (b + 1) * span]
        top = top_in[b * span : (b + 1) * span][:, 0:1]
        sc = nt(qh, cart_k) * two
        both = jnp.maximum(top, jnp.max(sc, axis=1, keepdims=True))
        wc = jnp.exp2(sc - both).astype(bf16)
        full = acc * jnp.exp2(top - both) + nn(wc, cart_vx)
        res = (full[:, :hd] / full[:, hd:]).astype(bf16)
        for n, h in enumerate(heads):
            out[:, h * hd : (h + 1) * hd] = res[n * rows : (n + 1) * rows]


VMEM = pl.BlockSpec(memory_space=pltpu.VMEM)


def call(body, outs, n_in, scratch=(), limit=40):
    return pl.pallas_call(
        body,
        out_shape=outs,
        in_specs=[VMEM] * n_in,
        out_specs=tuple(VMEM for _ in outs),
        scratch_shapes=list(scratch),
        compiler_params=pltpu.CompilerParams(vmem_limit_bytes=limit * 2**20),
    )


def local(sizes, queries, targets, document_keys, document_values, doc_pos, cart_keys, cartridge_values, master, first_moment1, second_moment2):
    n_dp, n_ctx, n_head = sizes
    hd = document_keys.shape[2]
    rows = queries.shape[1]
    group = queries.shape[2] // hd
    crows = cart_keys.shape[0]
    scale = hd ** (-0.5)
    per = math.gcd(group, 4)
    steps, dp_steps, head_steps = xor_steps(n_ctx), xor_steps(n_dp), xor_steps(n_head)
    sds = jax.ShapeDtypeStruct
    stride = 2 * rows + 2 * crows + 16
    masks = [0]
    for s in steps:
        masks += [m ^ s for m in masks]
    msg, st = pl.pallas_call(
        pack_kernel,
        out_shape=(sds((stride, hd), bf16), sds((3 * crows, master.shape[2]), f32)),
        in_specs=[pl.BlockSpec(memory_space=pltpu.HBM)] * 8,
        out_specs=(VMEM, VMEM),
        scratch_shapes=[pltpu.VMEM(doc_pos.shape, jnp.int32), pltpu.SemaphoreType.DMA((8,))],
        compiler_params=pltpu.CompilerParams(vmem_limit_bytes=8 * 2**20),
    )(
        *(
            pltpu.with_memory_space_constraint(x, pltpu.HBM)
            for x in (document_keys, document_values, doc_pos, cart_keys, cartridge_values, master, first_moment1, second_moment2)
        )
    )
    q, t = queries[0], targets[0]
    cart = n_ctx * crows
    shapes = (sds((rows * group, 2 * hd), f32), sds((rows * group, hd), f32))

    def chunk(msgs, state):
        body = functools.partial(chunk_kernel, len(msgs), scale, per, rows, stride)
        return call(body, shapes, 2 + len(msgs) + len(state))(q, msg, *msgs, *state)

    last = steps[-1:]
    pieces, mirrored, state = [msg], [], ()
    waiting = [msg]
    held = msg
    for s in steps[:-1]:
        piece = swap(held, "ctx", s, n_ctx)
        mirrored += [swap(pieces[-1], "ctx", m, n_ctx) for m in last]
        state = chunk(waiting, state)
        waiting = [piece, mirrored[-1]]
        held = jnp.concatenate([held, piece], axis=0)
        pieces.append(piece)
    if last:
        mirrored += [swap(pieces[-1], "ctx", last[0], n_ctx)]
        state = chunk(waiting, state)
        waiting = [mirrored[-1]]
    else:
        state = chunk(waiting, state)
        waiting = []
    for axis, s, size in [("dp", s, n_dp) for s in dp_steps] + [("ctx", s, n_ctx) for s in steps]:
        st = jnp.concatenate([st, swap(st, axis, s, size)], axis=0)
    msgs = pieces + mirrored
    acc, top, grad = call(
        functools.partial(gradient_kernel, len(waiting), masks, scale, per, rows, stride),
        shapes + (sds((cart, 2 * hd), bf16),),
        4 + len(msgs),
    )(q, t, *state, *msgs)
    chain = [("dp", s, n_dp) for s in dp_steps] + [("ctx", s, n_ctx) for s in steps]
    for n, (axis, s, size) in enumerate(chain):
        other = swap(grad, axis, s, size)
        if n + 1 < len(chain):
            grad = (grad.astype(f32) + other.astype(f32)).astype(bf16)
    total, squares = call(square_kernel, (sds((cart, 2 * hd), f32), sds((8, hd), f32)), 2)(grad, other)
    mine = squares
    theirs = jnp.zeros_like(squares)
    for n, s in enumerate(head_steps):
        if n:
            mine = mine + theirs
        theirs = swap(mine, "head", s, n_head)
    count = master.size * n_dp * n_ctx * n_head
    new_out, new_master, new_m1, new_m2 = call(
        functools.partial(final_kernel, masks, dp_steps, scale, per, count),
        (sds((rows, group * hd), bf16), sds(master.shape, f32), sds(master.shape, f32), sds(master.shape, f32)),
        10,
        [pltpu.VMEM((cart, 2 * hd), bf16)],
    )(q, acc, top, total, mine, theirs, st, master, first_moment1, second_moment2)
    return (new_out[None], new_master, new_m1, new_m2)


def solution(mesh):
    in_specs = (
        P("dp", "ctx", "head"),
        P("dp", "ctx", "head"),
        P("dp", "ctx", "head"),
        P("dp", "ctx", "head"),
        P("dp", "ctx"),
        P("ctx", "head"),
        P("ctx", "head"),
        P("ctx", "head", "dp"),
        P("ctx", "head", "dp"),
        P("ctx", "head", "dp"),
    )
    out_specs = (
        P("dp", "ctx", "head"),
        P("ctx", "head", "dp"),
        P("ctx", "head", "dp"),
        P("ctx", "head", "dp"),
    )
    sizes = (mesh.shape["dp"], mesh.shape["ctx"], mesh.shape["head"])

    def step(*args):
        return local(sizes, *args)

    return jax.shard_map(step, mesh=mesh, in_specs=in_specs, out_specs=out_specs, check_vma=False)
```

```python
import functools
import math

import jax
import jax.numpy as jnp
from jax import lax
from jax.experimental import pallas as pl
from jax.experimental.pallas import tpu as pltpu
from jax.sharding import PartitionSpec as P


beta_one = 0.8
beta_two = 0.95
learn_rate = 0.1
adam_eps = 1e-08
norm_eps = 1e-06
neg_big = -1e30
log2_e = math.log2(math.e)
pos_base = 256.0
f32, bf16 = jnp.float32, jnp.bfloat16


def xor_steps(size):
    assert size & (size - 1) == 0
    return [1 << b for b in reversed(range(size.bit_length() - 1))]


def swap(x, axis, mask, size):
    return lax.ppermute(x, axis, [(i, i ^ mask) for i in range(size)])


def place(mask, steps):
    at = 0
    for n, step in enumerate(steps):
        bit = step.bit_length() - 1
        at = at + (((mask >> bit) & 1) << n)
    return at


def nt(a, b):
    return lax.dot_general(a, b, (((1,), (1,)), ((), ())), preferred_element_type=f32)


def tn(a, b):
    return lax.dot_general(a, b, (((0,), (0,)), ((), ())), preferred_element_type=f32)


def nn(a, b):
    return jnp.dot(a, b, preferred_element_type=f32)


def pack_kernel(k, v, pos, ck, cv, ma, m1, m2, msg, st, line, sems):
    rows, crows, hd = k.shape[1], ck.shape[0], k.shape[2]
    at = 2 * rows
    copies = [
        (k.at[0], msg.at[0:rows]),
        (v.at[0], msg.at[rows:at]),
        (ck, msg.at[at : at + crows]),
        (cv, msg.at[at + crows : at + 2 * crows]),
        (pos, line),
    ]
    copies += [(ref.at[:, 0, :], st.at[n * crows : (n + 1) * crows]) for n, ref in enumerate((ma, m1, m2))]
    started = [pltpu.make_async_copy(x, y, sems.at[n]) for n, (x, y) in enumerate(copies)]
    for copy in started:
        copy.start()
    for copy in started:
        copy.wait()
    at += 2 * crows
    p = line[...].astype(f32)
    hi = jnp.floor(p * (1.0 / pos_base))
    lo = p - hi * pos_base
    row = lax.broadcasted_iota(jnp.int32, (16, hd), 0)
    both = jnp.where(row == 0, jnp.broadcast_to(hi, (16, hd)), jnp.broadcast_to(lo, (16, hd)))
    msg[at : at + 16] = both.astype(bf16)


def split(refs, stride):
    return [(ref, j * stride) for ref in refs for j in range(ref.shape[0] // stride)]


def positions(ref, at, stride):
    two_rows = ref[at + stride - 16 : at + stride].astype(f32)
    return two_rows[0:1] * pos_base + two_rows[1:2]


def document_part(own, blocks, rows, stride):
    query_pos = jnp.broadcast_to(positions(own, 0, stride), (rows, rows))
    keys, values = [], []
    for ref, at in blocks:
        key_pos = jnp.broadcast_to(positions(ref, at, stride), (rows, rows)).T
        barred = jnp.where(key_pos <= query_pos, 0.0, neg_big).astype(bf16)
        keys.append(jnp.concatenate([ref[at : at + rows], barred], axis=1))
        values.append(ref[at + rows : at + 2 * rows])
    values = jnp.concatenate(values, axis=0)
    return jnp.concatenate(keys, axis=0), jnp.concatenate([values, jnp.ones_like(values)], axis=1)


def heads_of(ref, b, per, hd):
    return jnp.concatenate([ref[:, h * hd : (h + 1) * hd] for h in range(b * per, (b + 1) * per)], axis=0)


def pick(rows, per):
    line = lax.broadcasted_iota(jnp.int32, (rows, rows), 0)
    lane = lax.broadcasted_iota(jnp.int32, (rows, rows), 1)
    one = jnp.where(line == lane, 1.0, 0.0).astype(bf16)
    return jnp.concatenate([one] * per, axis=0)


def wide(x, columns):
    return jnp.concatenate([x] * (columns // x.shape[1]), axis=1)


def attend(qx, part, two, state):
    keys, values = part
    s = nt(qx, keys) * two
    top = jnp.max(s, axis=1, keepdims=True)
    hd = values.shape[1] // 2
    if state is None:
        top = jnp.broadcast_to(top, (s.shape[0], hd))
        both = nn(jnp.exp2(s - wide(top, s.shape[1])).astype(bf16), values)
        return both[:, :hd], both[:, hd:], top
    acc, total, old = state
    top = jnp.maximum(old, top)
    both = nn(jnp.exp2(s - wide(top, s.shape[1])).astype(bf16), values)
    keep = jnp.exp2(old - top)
    return acc * keep + both[:, :hd], total * keep + both[:, hd:], top


def chunk_kernel(n_msgs, scale, per, rows, stride, *refs):
    q, own, msgs = refs[0], refs[1], refs[2 : 2 + n_msgs]
    outs = refs[2 + n_msgs :]
    hd = own.shape[1]
    part = document_part(own, split(msgs, stride), rows, stride)
    eye = pick(rows, per)
    span = per * rows
    for b in range(q.shape[1] // hd // per):
        cut = slice(b * span, (b + 1) * span)
        qx = jnp.concatenate([heads_of(q, b, per, hd), eye], axis=1)
        for ref, x in zip(outs, attend(qx, part, scale * log2_e, None)):
            ref[cut] = x


def gradient_kernel(n_last, masks, scale, per, rows, stride, *refs):
    q, t = refs[:2]
    olds = refs[2:5]
    outs, grad = refs[-4:-1], refs[-1]
    msgs = refs[5:-4]
    own = msgs[0]
    hd = own.shape[1]
    crows = (stride - 2 * rows - 16) // 2
    me = lax.axis_index("ctx")
    two = scale * log2_e
    part = document_part(own, split(msgs[len(msgs) - n_last :], stride), rows, stride)
    every = [(ref, at + 2 * rows) for ref, at in split(msgs, stride)]
    cart_k = jnp.concatenate([ref[at : at + crows] for ref, at in every], axis=0)
    cart_v = jnp.concatenate([ref[at + crows : at + 2 * crows] for ref, at in every], axis=0)
    cart_vx = jnp.concatenate([cart_v, jnp.ones_like(cart_v)], axis=1)
    n_cart = cart_k.shape[0]
    eye = pick(rows, per)
    span = per * rows
    gk = jnp.zeros((n_cart, hd), f32)
    gv = jnp.zeros((n_cart, hd), f32)
    for b in range(q.shape[1] // hd // per):
        cut = slice(b * span, (b + 1) * span)
        qh = heads_of(q, b, per, hd)
        acc, total, top = attend(jnp.concatenate([qh, eye], axis=1), part, two, tuple(ref[cut] for ref in olds))
        for ref, x in zip(outs, (acc, total, top)):
            ref[cut] = x
        sc = nt(qh, cart_k) * two
        both = jnp.maximum(top, jnp.max(sc, axis=1, keepdims=True))
        wc = jnp.exp2(sc - wide(both, n_cart))
        keep = jnp.exp2(top - both)
        more = nn(wc.astype(bf16), cart_vx)
        inv = 1.0 / (total * keep + more[:, hd:])
        out = (acc * keep + more[:, :hd]) * inv
        d_out = out - heads_of(t, b, per, hd).astype(f32)
        delta = jnp.sum(d_out * out, axis=1, keepdims=True)
        d_out_b = d_out.astype(bf16)
        probs = wc * wide(inv, n_cart)
        ds = probs * (nt(d_out_b, cart_v) - delta)
        gk = gk + tn(ds.astype(bf16), qh)
        gv = gv + tn(probs.astype(bf16), d_out_b)
    whole = jnp.concatenate([gk * scale, gv], axis=1).astype(bf16)
    for j, mask in enumerate(masks):
        to = pl.multiple_of((me ^ mask) * crows, crows)
        grad[pl.ds(to, crows)] = whole[j * crows : (j + 1) * crows]


def square_kernel(a, b, total, squares):
    g = a[...].astype(f32) + b[...].astype(f32)
    total[...] = g
    squares[...] = jnp.broadcast_to(jnp.sum(g * g, keepdims=True), squares.shape)


def update(g, ma, m1, m2):
    one = beta_one * m1 + (1.0 - beta_one) * g
    two = beta_two * m2 + (1.0 - beta_two) * g * g
    return one, two, ma - learn_rate * one / (jnp.sqrt(two) + adam_eps)


def final_kernel(masks, dp_steps, scale, per, count, q, acc_in, total_in, top_in, g, sq_a, sq_b, st, ma, m1, m2, out, ma_o, m1_o, m2_o, cart):
    rows, hd = q.shape[0], acc_in.shape[1]
    group = q.shape[1] // hd
    n_dp = 1 << len(dp_steps)
    crows, width = ma.shape[0], ma.shape[2]
    me, my_dp = lax.axis_index("ctx"), lax.axis_index("dp")
    two = scale * log2_e
    mean = (sq_a[0:1, 0:1] + sq_b[0:1, 0:1]) * (1.0 / count)
    inv_rms = 1.0 / jnp.sqrt(mean + norm_eps)
    mine = g[pl.ds(pl.multiple_of(me * crows, crows), crows)]
    own = mine[:, 0:width]
    for d in range(1, n_dp):
        own = jnp.where(my_dp == d, mine[:, d * width : (d + 1) * width], own)
    one, sec, new = update(own * inv_rms, ma[:, 0, :], m1[:, 0, :], m2[:, 0, :])
    m1_o[:, 0, :] = one
    m2_o[:, 0, :] = sec
    ma_o[:, 0, :] = new
    for r, mask in enumerate(masks):
        parts = [[], [], []]
        for d in range(n_dp):
            at = (r * n_dp + place(my_dp ^ d, dp_steps)) * 3 * crows
            for n in range(3):
                parts[n].append(st[pl.ds(pl.multiple_of(at + n * crows, crows), crows)])
        ma_r, m1_r, m2_r = (jnp.concatenate(x, axis=1) for x in parts)
        rows_g = g[pl.ds(pl.multiple_of((me ^ mask) * crows, crows), crows)]
        _, _, new = update(rows_g * inv_rms, ma_r, m1_r, m2_r)
        cart[r * crows : (r + 1) * crows] = new.astype(bf16)
    cart_k = cart[:, :hd]
    cart_v = cart[:, hd:]
    cart_vx = jnp.concatenate([cart_v, jnp.ones_like(cart_v)], axis=1)
    span = per * rows
    for b in range(group // per):
        heads = range(b * per, (b + 1) * per)
        qh = jnp.concatenate([q[:, h * hd : (h + 1) * hd] for h in heads], axis=0)
        cut = slice(b * span, (b + 1) * span)
        top = top_in[cut]
        sc = nt(qh, cart_k) * two
        both = jnp.maximum(top, jnp.max(sc, axis=1, keepdims=True))
        wc = jnp.exp2(sc - wide(both, sc.shape[1])).astype(bf16)
        keep = jnp.exp2(top - both)
        more = nn(wc, cart_vx)
        res = ((acc_in[cut] * keep + more[:, :hd]) / (total_in[cut] * keep + more[:, hd:])).astype(bf16)
        for n, h in enumerate(heads):
            out[:, h * hd : (h + 1) * hd] = res[n * rows : (n + 1) * rows]


VMEM = pl.BlockSpec(memory_space=pltpu.VMEM)


def call(body, outs, n_in, scratch=(), limit=40):
    return pl.pallas_call(
        body,
        out_shape=outs,
        in_specs=[VMEM] * n_in,
        out_specs=tuple(VMEM for _ in outs),
        scratch_shapes=list(scratch),
        compiler_params=pltpu.CompilerParams(vmem_limit_bytes=limit * 2**20),
    )


def local(sizes, queries, targets, document_keys, document_values, doc_pos, cart_keys, cartridge_values, master, first_moment1, second_moment2):
    n_dp, n_ctx, n_head = sizes
    hd = document_keys.shape[2]
    rows = queries.shape[1]
    group = queries.shape[2] // hd
    crows = cart_keys.shape[0]
    scale = hd ** (-0.5)
    per = math.gcd(group, 4)
    steps, dp_steps, head_steps = xor_steps(n_ctx), xor_steps(n_dp), xor_steps(n_head)
    sds = jax.ShapeDtypeStruct
    stride = 2 * rows + 2 * crows + 16
    masks = [0]
    for s in steps:
        masks += [m ^ s for m in masks]
    msg, st = pl.pallas_call(
        pack_kernel,
        out_shape=(sds((stride, hd), bf16), sds((3 * crows, master.shape[2]), f32)),
        in_specs=[pl.BlockSpec(memory_space=pltpu.HBM)] * 8,
        out_specs=(VMEM, VMEM),
        scratch_shapes=[pltpu.VMEM(doc_pos.shape, jnp.int32), pltpu.SemaphoreType.DMA((8,))],
        compiler_params=pltpu.CompilerParams(vmem_limit_bytes=8 * 2**20),
    )(
        *(
            pltpu.with_memory_space_constraint(x, pltpu.HBM)
            for x in (document_keys, document_values, doc_pos, cart_keys, cartridge_values, master, first_moment1, second_moment2)
        )
    )
    q, t = queries[0], targets[0]
    cart = n_ctx * crows
    shapes = (sds((rows * group, hd), f32),) * 3
    last = steps[-1]
    pieces, mirrored, held = [msg], [], msg
    for s in steps[:-1]:
        piece = swap(held, "ctx", s, n_ctx)
        mirrored.append(swap(pieces[-1], "ctx", last, n_ctx))
        held = jnp.concatenate([held, piece], axis=0)
        pieces.append(piece)
    mirrored.append(swap(pieces[-1], "ctx", last, n_ctx))
    msgs = pieces + mirrored
    body = functools.partial(chunk_kernel, len(msgs) - 1, scale, per, rows, stride)
    state = call(body, shapes, 1 + len(msgs))(q, msg, *msgs[:-1])
    for axis, s, size in [("dp", s, n_dp) for s in dp_steps] + [("ctx", s, n_ctx) for s in steps]:
        more = swap(st, axis, s, size)
        st = jnp.concatenate([st, more], axis=0)
    body = functools.partial(gradient_kernel, 1, masks, scale, math.gcd(group, 8), rows, stride)
    *state, grad = call(body, shapes + (sds((cart, 2 * hd), bf16),), 5 + len(msgs))(q, t, *state, *msgs)
    chain = [("dp", s, n_dp) for s in dp_steps] + [("ctx", s, n_ctx) for s in steps]
    for n, (axis, s, size) in enumerate(chain):
        other = swap(grad, axis, s, size)
        if n + 1 < len(chain):
            grad = (grad.astype(f32) + other.astype(f32)).astype(bf16)
    total, squares = call(square_kernel, (sds((cart, 2 * hd), f32), sds((8, hd), f32)), 2)(grad, other)
    mine = squares
    theirs = jnp.zeros_like(squares)
    for n, s in enumerate(head_steps):
        if n:
            mine = mine + theirs
        theirs = swap(mine, "head", s, n_head)
    count = master.size * n_dp * n_ctx * n_head
    new_out, new_master, new_m1, new_m2 = call(
        functools.partial(final_kernel, masks, dp_steps, scale, per, count),
        (sds((rows, group * hd), bf16), sds(master.shape, f32), sds(master.shape, f32), sds(master.shape, f32)),
        11,
        [pltpu.VMEM((cart, 2 * hd), bf16)],
    )(q, *state, total, mine, theirs, st, master, first_moment1, second_moment2)
    return (new_out[None], new_master, new_m1, new_m2)


def solution(mesh):
    in_specs = (
        P("dp", "ctx", "head"),
        P("dp", "ctx", "head"),
        P("dp", "ctx", "head"),
        P("dp", "ctx", "head"),
        P("dp", "ctx"),
        P("ctx", "head"),
        P("ctx", "head"),
        P("ctx", "head", "dp"),
        P("ctx", "head", "dp"),
        P("ctx", "head", "dp"),
    )
    out_specs = (
        P("dp", "ctx", "head"),
        P("ctx", "head", "dp"),
        P("ctx", "head", "dp"),
        P("ctx", "head", "dp"),
    )
    sizes = (mesh.shape["dp"], mesh.shape["ctx"], mesh.shape["head"])

    def step(*args):
        return local(sizes, *args)

    return jax.shard_map(step, mesh=mesh, in_specs=in_specs, out_specs=out_specs, check_vma=False)
```

```python
import functools
import math

import jax
import jax.numpy as jnp
from jax import lax
from jax.experimental import pallas as pl
from jax.experimental.pallas import tpu as pltpu
from jax.sharding import PartitionSpec as P


beta_one = 0.8
beta_two = 0.95
learn_rate = 0.1
adam_eps = 1e-08
norm_eps = 1e-06
neg_big = -1e30
log2_e = math.log2(math.e)
pos_base = 256.0
f32, bf16 = jnp.float32, jnp.bfloat16


def xor_steps(size):
    assert size & (size - 1) == 0
    return [1 << b for b in reversed(range(size.bit_length() - 1))]


def swap(x, axis, mask, size):
    return lax.ppermute(x, axis, [(i, i ^ mask) for i in range(size)])


def spot(chain, axis, mask):
    at = 0
    for n, (name, step) in enumerate(chain):
        if name == axis:
            at = at + (((mask >> (step.bit_length() - 1)) & 1) << n)
    return at


def nt(a, b):
    return lax.dot_general(a, b, (((1,), (1,)), ((), ())), preferred_element_type=f32)


def tn(a, b):
    return lax.dot_general(a, b, (((0,), (0,)), ((), ())), preferred_element_type=f32)


def nn(a, b):
    return jnp.dot(a, b, preferred_element_type=f32)


def pack_kernel(k, v, pos, ck, cv, ma, m1, m2, msg, st, line, sems):
    rows, crows, hd = k.shape[1], ck.shape[0], k.shape[2]
    at = 2 * rows
    copies = [
        (k.at[0], msg.at[0:rows]),
        (v.at[0], msg.at[rows:at]),
        (ck, msg.at[at : at + crows]),
        (cv, msg.at[at + crows : at + 2 * crows]),
        (pos, line),
    ]
    copies += [(ref.at[:, 0, :], st.at[n * crows : (n + 1) * crows]) for n, ref in enumerate((ma, m1, m2))]
    started = [pltpu.make_async_copy(x, y, sems.at[n]) for n, (x, y) in enumerate(copies)]
    for copy in started:
        copy.start()
    for copy in started:
        copy.wait()
    at += 2 * crows
    p = line[...].astype(f32)
    hi = jnp.floor(p * (1.0 / pos_base))
    lo = p - hi * pos_base
    row = lax.broadcasted_iota(jnp.int32, (16, hd), 0)
    both = jnp.where(row == 0, jnp.broadcast_to(hi, (16, hd)), jnp.broadcast_to(lo, (16, hd)))
    msg[at : at + 16] = both.astype(bf16)


def split(refs, stride):
    return [(ref, j * stride) for ref in refs for j in range(ref.shape[0] // stride)]


def positions(ref, at, stride):
    two_rows = ref[at + stride - 16 : at + stride].astype(f32)
    return two_rows[0:1] * pos_base + two_rows[1:2]


def document_part(own, blocks, rows, stride):
    query_pos = jnp.broadcast_to(positions(own, 0, stride), (rows, rows))
    keys, values = [], []
    for ref, at in blocks:
        key_pos = jnp.broadcast_to(positions(ref, at, stride), (rows, rows)).T
        barred = jnp.where(key_pos <= query_pos, 0.0, neg_big).astype(bf16)
        keys.append(jnp.concatenate([ref[at : at + rows], barred], axis=1))
        values.append(ref[at + rows : at + 2 * rows])
    values = jnp.concatenate(values, axis=0)
    return jnp.concatenate(keys, axis=0), jnp.concatenate([values, jnp.ones_like(values)], axis=1)


def heads_of(ref, b, per, hd):
    return jnp.concatenate([ref[:, h * hd : (h + 1) * hd] for h in range(b * per, (b + 1) * per)], axis=0)


def pick(rows, per):
    line = lax.broadcasted_iota(jnp.int32, (rows, rows), 0)
    lane = lax.broadcasted_iota(jnp.int32, (rows, rows), 1)
    one = jnp.where(line == lane, 1.0, 0.0).astype(bf16)
    return jnp.concatenate([one] * per, axis=0)


def wide(x, columns):
    return jnp.concatenate([x] * (columns // x.shape[1]), axis=1)


def attend(qx, part, two, state):
    keys, values = part
    s = nt(qx, keys) * two
    top = jnp.max(s, axis=1, keepdims=True)
    hd = values.shape[1] // 2
    if state is None:
        top = jnp.broadcast_to(top, (s.shape[0], hd))
        both = nn(jnp.exp2(s - wide(top, s.shape[1])).astype(bf16), values)
        return both[:, :hd], both[:, hd:], top
    acc, total, old = state
    top = jnp.maximum(old, top)
    both = nn(jnp.exp2(s - wide(top, s.shape[1])).astype(bf16), values)
    keep = jnp.exp2(old - top)
    return acc * keep + both[:, :hd], total * keep + both[:, hd:], top


def chunk_kernel(n_msgs, scale, per, rows, stride, *refs):
    q, own, msgs = refs[0], refs[1], refs[2 : 2 + n_msgs]
    outs = refs[2 + n_msgs :]
    hd = own.shape[1]
    part = document_part(own, split(msgs, stride), rows, stride)
    eye = pick(rows, per)
    span = per * rows
    for b in range(q.shape[1] // hd // per):
        cut = slice(b * span, (b + 1) * span)
        qx = jnp.concatenate([heads_of(q, b, per, hd), eye], axis=1)
        for ref, x in zip(outs, attend(qx, part, scale * log2_e, None)):
            ref[cut] = x


def gradient_kernel(n_last, masks, scale, per, rows, stride, *refs):
    q, t = refs[:2]
    olds = refs[2:5]
    outs, grad = refs[-4:-1], refs[-1]
    msgs = refs[5:-4]
    own = msgs[0]
    hd = own.shape[1]
    crows = (stride - 2 * rows - 16) // 2
    me = lax.axis_index("ctx")
    two = scale * log2_e
    part = document_part(own, split(msgs[len(msgs) - n_last :], stride), rows, stride)
    every = [(ref, at + 2 * rows) for ref, at in split(msgs, stride)]
    cart_k = jnp.concatenate([ref[at : at + crows] for ref, at in every], axis=0)
    cart_v = jnp.concatenate([ref[at + crows : at + 2 * crows] for ref, at in every], axis=0)
    cart_vx = jnp.concatenate([cart_v, jnp.ones_like(cart_v)], axis=1)
    n_cart = cart_k.shape[0]
    eye = pick(rows, per)
    span = per * rows
    gk = jnp.zeros((n_cart, hd), f32)
    gv = jnp.zeros((n_cart, hd), f32)
    for b in range(q.shape[1] // hd // per):
        cut = slice(b * span, (b + 1) * span)
        qh = heads_of(q, b, per, hd)
        acc, total, top = attend(jnp.concatenate([qh, eye], axis=1), part, two, tuple(ref[cut] for ref in olds))
        for ref, x in zip(outs, (acc, total, top)):
            ref[cut] = x
        sc = nt(qh, cart_k) * two
        both = jnp.maximum(top, jnp.max(sc, axis=1, keepdims=True))
        wc = jnp.exp2(sc - wide(both, n_cart))
        keep = jnp.exp2(top - both)
        more = nn(wc.astype(bf16), cart_vx)
        inv = 1.0 / (total * keep + more[:, hd:])
        out = (acc * keep + more[:, :hd]) * inv
        d_out = out - heads_of(t, b, per, hd).astype(f32)
        delta = jnp.sum(d_out * out, axis=1, keepdims=True)
        d_out_b = d_out.astype(bf16)
        probs = wc * wide(inv, n_cart)
        ds = probs * (nt(d_out_b, cart_v) - delta)
        gk = gk + tn(ds.astype(bf16), qh)
        gv = gv + tn(probs.astype(bf16), d_out_b)
    whole = jnp.concatenate([gk * scale, gv], axis=1).astype(bf16)
    for j, mask in enumerate(masks):
        to = pl.multiple_of((me ^ mask) * crows, crows)
        grad[pl.ds(to, crows)] = whole[j * crows : (j + 1) * crows]


def summed(parts):
    parts = [x.astype(f32) for x in parts]
    if len(parts) == 2:
        return parts[0] + parts[1]
    own, one, two, both = parts
    return (own + both) + (one + two)


def square_kernel(*refs):
    total, squares = refs[-2:]
    g = summed([ref[...] for ref in refs[:-2]])
    total[...] = g
    squares[...] = jnp.broadcast_to(jnp.sum(g * g, keepdims=True), squares.shape)


def update(g, ma, m1, m2):
    one = beta_one * m1 + (1.0 - beta_one) * g
    two = beta_two * m2 + (1.0 - beta_two) * g * g
    return one, two, ma - learn_rate * one / (jnp.sqrt(two) + adam_eps)


def final_kernel(masks, chain, n_dp, scale, per, count, q, acc_in, total_in, top_in, g, sq_a, sq_b, st, ma, m1, m2, out, ma_o, m1_o, m2_o, cart):
    rows, hd = q.shape[0], acc_in.shape[1]
    group = q.shape[1] // hd
    crows, width = ma.shape[0], ma.shape[2]
    me, my_dp = lax.axis_index("ctx"), lax.axis_index("dp")
    two = scale * log2_e
    mean = (sq_a[0:1, 0:1] + sq_b[0:1, 0:1]) * (1.0 / count)
    inv_rms = 1.0 / jnp.sqrt(mean + norm_eps)
    mine = g[pl.ds(pl.multiple_of(me * crows, crows), crows)]
    own = mine[:, 0:width]
    for d in range(1, n_dp):
        own = jnp.where(my_dp == d, mine[:, d * width : (d + 1) * width], own)
    one, sec, new = update(own * inv_rms, ma[:, 0, :], m1[:, 0, :], m2[:, 0, :])
    m1_o[:, 0, :] = one
    m2_o[:, 0, :] = sec
    ma_o[:, 0, :] = new
    for r, mask in enumerate(masks):
        parts = [[], [], []]
        for d in range(n_dp):
            at = (spot(chain, "ctx", mask) + spot(chain, "dp", my_dp ^ d)) * 3 * crows
            for n in range(3):
                parts[n].append(st[pl.ds(pl.multiple_of(at + n * crows, crows), crows)])
        ma_r, m1_r, m2_r = (jnp.concatenate(x, axis=1) for x in parts)
        rows_g = g[pl.ds(pl.multiple_of((me ^ mask) * crows, crows), crows)]
        _, _, new = update(rows_g * inv_rms, ma_r, m1_r, m2_r)
        cart[r * crows : (r + 1) * crows] = new.astype(bf16)
    cart_k = cart[:, :hd]
    cart_v = cart[:, hd:]
    cart_vx = jnp.concatenate([cart_v, jnp.ones_like(cart_v)], axis=1)
    span = per * rows
    for b in range(group // per):
        heads = range(b * per, (b + 1) * per)
        qh = jnp.concatenate([q[:, h * hd : (h + 1) * hd] for h in heads], axis=0)
        cut = slice(b * span, (b + 1) * span)
        top = top_in[cut]
        sc = nt(qh, cart_k) * two
        both = jnp.maximum(top, jnp.max(sc, axis=1, keepdims=True))
        wc = jnp.exp2(sc - wide(both, sc.shape[1])).astype(bf16)
        keep = jnp.exp2(top - both)
        more = nn(wc, cart_vx)
        res = ((acc_in[cut] * keep + more[:, :hd]) / (total_in[cut] * keep + more[:, hd:])).astype(bf16)
        for n, h in enumerate(heads):
            out[:, h * hd : (h + 1) * hd] = res[n * rows : (n + 1) * rows]


VMEM = pl.BlockSpec(memory_space=pltpu.VMEM)


def call(body, outs, n_in, scratch=(), limit=40):
    return pl.pallas_call(
        body,
        out_shape=outs,
        in_specs=[VMEM] * n_in,
        out_specs=tuple(VMEM for _ in outs),
        scratch_shapes=list(scratch),
        compiler_params=pltpu.CompilerParams(vmem_limit_bytes=limit * 2**20),
    )


def local(sizes, queries, targets, document_keys, document_values, doc_pos, cart_keys, cartridge_values, master, first_moment1, second_moment2):
    n_dp, n_ctx, n_head = sizes
    hd = document_keys.shape[2]
    rows = queries.shape[1]
    group = queries.shape[2] // hd
    crows = cart_keys.shape[0]
    scale = hd ** (-0.5)
    per = math.gcd(group, 4)
    steps, dp_steps, head_steps = xor_steps(n_ctx), xor_steps(n_dp), xor_steps(n_head)
    sds = jax.ShapeDtypeStruct
    stride = 2 * rows + 2 * crows + 16
    masks = [0]
    for s in steps:
        masks += [m ^ s for m in masks]
    msg, st = pl.pallas_call(
        pack_kernel,
        out_shape=(sds((stride, hd), bf16), sds((3 * crows, master.shape[2]), f32)),
        in_specs=[pl.BlockSpec(memory_space=pltpu.HBM)] * 8,
        out_specs=(VMEM, VMEM),
        scratch_shapes=[pltpu.VMEM(doc_pos.shape, jnp.int32), pltpu.SemaphoreType.DMA((8,))],
        compiler_params=pltpu.CompilerParams(vmem_limit_bytes=8 * 2**20),
    )(
        *(
            pltpu.with_memory_space_constraint(x, pltpu.HBM)
            for x in (document_keys, document_values, doc_pos, cart_keys, cartridge_values, master, first_moment1, second_moment2)
        )
    )
    q, t = queries[0], targets[0]
    cart = n_ctx * crows
    shapes = (sds((rows * group, hd), f32),) * 3
    last = steps[-1]
    pieces, mirrored, held = [msg], [], msg
    for s in steps[:-1]:
        piece = swap(held, "ctx", s, n_ctx)
        mirrored.append(swap(pieces[-1], "ctx", last, n_ctx))
        held = jnp.concatenate([held, piece], axis=0)
        pieces.append(piece)
    mirrored.append(swap(pieces[-1], "ctx", last, n_ctx))
    msgs = pieces + mirrored
    body = functools.partial(chunk_kernel, len(msgs) - 1, scale, per, rows, stride)
    state = call(body, shapes, 1 + len(msgs))(q, msg, *msgs[:-1])
    chain = [("ctx", s) for s in steps]
    chain[1:1] = [("dp", s) for s in dp_steps]
    for axis, s in chain:
        more = swap(st, axis, s, {"ctx": n_ctx, "dp": n_dp}[axis])
        st = jnp.concatenate([st, more], axis=0)
    body = functools.partial(gradient_kernel, 1, masks, scale, math.gcd(group, 8), rows, stride)
    *state, grad = call(body, shapes + (sds((cart, 2 * hd), bf16),), 5 + len(msgs))(q, t, *state, *msgs)
    bits = steps + [s * n_ctx for s in dp_steps]
    rounds = [bits[n : n + 2] for n in range(0, len(bits), 2)]
    for n, pair in enumerate(rounds):
        ways = pair + [sum(pair)] if len(pair) == 2 else pair
        others = [lax.ppermute(grad, ("dp", "ctx"), [(i, i ^ m) for i in range(n_dp * n_ctx)]) for m in ways]
        if n + 1 < len(rounds):
            grad = summed([grad] + others).astype(bf16)
    total, squares = call(square_kernel, (sds((cart, 2 * hd), f32), sds((8, hd), f32)), 1 + len(others))(grad, *others)
    mine = squares
    theirs = jnp.zeros_like(squares)
    for n, s in enumerate(head_steps):
        if n:
            mine = mine + theirs
        theirs = swap(mine, "head", s, n_head)
    count = master.size * n_dp * n_ctx * n_head
    new_out, new_master, new_m1, new_m2 = call(
        functools.partial(final_kernel, masks, chain, n_dp, scale, per, count),
        (sds((rows, group * hd), bf16), sds(master.shape, f32), sds(master.shape, f32), sds(master.shape, f32)),
        11,
        [pltpu.VMEM((cart, 2 * hd), bf16)],
    )(q, *state, total, mine, theirs, st, master, first_moment1, second_moment2)
    return (new_out[None], new_master, new_m1, new_m2)


def solution(mesh):
    in_specs = (
        P("dp", "ctx", "head"),
        P("dp", "ctx", "head"),
        P("dp", "ctx", "head"),
        P("dp", "ctx", "head"),
        P("dp", "ctx"),
        P("ctx", "head"),
        P("ctx", "head"),
        P("ctx", "head", "dp"),
        P("ctx", "head", "dp"),
        P("ctx", "head", "dp"),
    )
    out_specs = (
        P("dp", "ctx", "head"),
        P("ctx", "head", "dp"),
        P("ctx", "head", "dp"),
        P("ctx", "head", "dp"),
    )
    sizes = (mesh.shape["dp"], mesh.shape["ctx"], mesh.shape["head"])

    def step(*args):
        return local(sizes, *args)

    return jax.shard_map(step, mesh=mesh, in_specs=in_specs, out_specs=out_specs, check_vma=False)
```

```python
import functools
import math

import jax
import jax.numpy as jnp
from jax import lax
from jax.experimental import pallas as pl
from jax.experimental.pallas import tpu as pltpu
from jax.sharding import PartitionSpec as P


beta_one = 0.8
beta_two = 0.95
learn_rate = 0.1
adam_eps = 1e-08
norm_eps = 1e-06
neg_big = -1e30
log2_e = math.log2(math.e)
pos_base = 256.0
f32, bf16 = jnp.float32, jnp.bfloat16


def xor_steps(size):
    assert size & (size - 1) == 0
    return [1 << b for b in reversed(range(size.bit_length() - 1))]


def swap(x, axis, mask, size):
    return lax.ppermute(x, axis, [(i, i ^ mask) for i in range(size)])


def joined(parts):
    return jnp.concatenate(parts, axis=0) if len(parts) > 1 else parts[0]


def spot(chain, axis, mask):
    at = 0
    for n, (name, step) in enumerate(chain):
        if name == axis:
            at = at + (((mask >> (step.bit_length() - 1)) & 1) << n)
    return at


def nt(a, b):
    return lax.dot_general(a, b, (((1,), (1,)), ((), ())), preferred_element_type=f32)


def tn(a, b):
    return lax.dot_general(a, b, (((0,), (0,)), ((), ())), preferred_element_type=f32)


def nn(a, b):
    return jnp.dot(a, b, preferred_element_type=f32)


def pack_kernel(k, v, pos, ck, cv, ma, m1, m2, msg, st, line, sems):
    rows, crows, hd = k.shape[1], ck.shape[0], k.shape[2]
    at = 2 * rows
    copies = [
        (k.at[0], msg.at[0:rows]),
        (v.at[0], msg.at[rows:at]),
        (ck, msg.at[at : at + crows]),
        (cv, msg.at[at + crows : at + 2 * crows]),
        (pos, line),
    ]
    copies += [(ref.at[:, 0, :], st.at[n * crows : (n + 1) * crows]) for n, ref in enumerate((ma, m1, m2))]
    started = [pltpu.make_async_copy(x, y, sems.at[n]) for n, (x, y) in enumerate(copies)]
    for copy in started:
        copy.start()
    for copy in started:
        copy.wait()
    at += 2 * crows
    p = line[...].astype(f32)
    hi = jnp.floor(p * (1.0 / pos_base))
    lo = p - hi * pos_base
    row = lax.broadcasted_iota(jnp.int32, (16, hd), 0)
    both = jnp.where(row == 0, jnp.broadcast_to(hi, (16, hd)), jnp.broadcast_to(lo, (16, hd)))
    msg[at : at + 16] = both.astype(bf16)


def split(refs, stride):
    return [(ref, j * stride) for ref in refs for j in range(ref.shape[0] // stride)]


def positions(ref, at, stride):
    two_rows = ref[at + stride - 16 : at + stride].astype(f32)
    return two_rows[0:1] * pos_base + two_rows[1:2]


def document_part(own, blocks, rows, stride):
    query_pos = jnp.broadcast_to(positions(own, 0, stride), (rows, rows))
    keys, values = [], []
    for ref, at in blocks:
        key_pos = jnp.broadcast_to(positions(ref, at, stride), (rows, rows)).T
        barred = jnp.where(key_pos <= query_pos, 0.0, neg_big).astype(bf16)
        keys.append(jnp.concatenate([ref[at : at + rows], barred], axis=1))
        values.append(ref[at + rows : at + 2 * rows])
    values = jnp.concatenate(values, axis=0)
    return jnp.concatenate(keys, axis=0), jnp.concatenate([values, jnp.ones_like(values)], axis=1)


def heads_of(ref, b, per, hd):
    return jnp.concatenate([ref[:, h * hd : (h + 1) * hd] for h in range(b * per, (b + 1) * per)], axis=0)


def pick(rows, per):
    line = lax.broadcasted_iota(jnp.int32, (rows, rows), 0)
    lane = lax.broadcasted_iota(jnp.int32, (rows, rows), 1)
    one = jnp.where(line == lane, 1.0, 0.0).astype(bf16)
    return jnp.concatenate([one] * per, axis=0)


def wide(x, columns):
    return jnp.concatenate([x] * (columns // x.shape[1]), axis=1)


def attend(qx, part, two, state):
    keys, values = part
    s = nt(qx, keys) * two
    top = jnp.max(s, axis=1, keepdims=True)
    hd = values.shape[1] // 2
    if state is None:
        top = jnp.broadcast_to(top, (s.shape[0], hd))
        both = nn(jnp.exp2(s - wide(top, s.shape[1])).astype(bf16), values)
        return both[:, :hd], both[:, hd:], top
    acc, total, old = state
    top = jnp.maximum(old, top)
    both = nn(jnp.exp2(s - wide(top, s.shape[1])).astype(bf16), values)
    keep = jnp.exp2(old - top)
    return acc * keep + both[:, :hd], total * keep + both[:, hd:], top


def chunk_kernel(n_msgs, scale, per, rows, stride, *refs):
    q, own, msgs = refs[0], refs[1], refs[2 : 2 + n_msgs]
    outs = refs[2 + n_msgs :]
    hd = own.shape[1]
    part = document_part(own, split(msgs, stride), rows, stride)
    eye = pick(rows, per)
    span = per * rows
    for b in range(q.shape[1] // hd // per):
        cut = slice(b * span, (b + 1) * span)
        qx = jnp.concatenate([heads_of(q, b, per, hd), eye], axis=1)
        for ref, x in zip(outs, attend(qx, part, scale * log2_e, None)):
            ref[cut] = x


def gradient_kernel(n_last, masks, scale, per, rows, stride, *refs):
    q, t = refs[:2]
    olds = refs[2:5]
    outs, grad = refs[-4:-1], refs[-1]
    msgs = refs[5:-4]
    own = msgs[0]
    hd = own.shape[1]
    crows = (stride - 2 * rows - 16) // 2
    me = lax.axis_index("ctx")
    two = scale * log2_e
    part = document_part(own, split(msgs[len(msgs) - n_last :], stride), rows, stride)
    every = [(ref, at + 2 * rows) for ref, at in split(msgs, stride)]
    cart_k = jnp.concatenate([ref[at : at + crows] for ref, at in every], axis=0)
    cart_v = jnp.concatenate([ref[at + crows : at + 2 * crows] for ref, at in every], axis=0)
    cart_vx = jnp.concatenate([cart_v, jnp.ones_like(cart_v)], axis=1)
    n_cart = cart_k.shape[0]
    eye = pick(rows, per)
    span = per * rows
    gk = jnp.zeros((n_cart, hd), f32)
    gv = jnp.zeros((n_cart, hd), f32)
    for b in range(q.shape[1] // hd // per):
        cut = slice(b * span, (b + 1) * span)
        qh = heads_of(q, b, per, hd)
        acc, total, top = attend(jnp.concatenate([qh, eye], axis=1), part, two, tuple(ref[cut] for ref in olds))
        for ref, x in zip(outs, (acc, total, top)):
            ref[cut] = x
        sc = nt(qh, cart_k) * two
        both = jnp.maximum(top, jnp.max(sc, axis=1, keepdims=True))
        wc = jnp.exp2(sc - wide(both, n_cart))
        keep = jnp.exp2(top - both)
        more = nn(wc.astype(bf16), cart_vx)
        inv = 1.0 / (total * keep + more[:, hd:])
        out = (acc * keep + more[:, :hd]) * inv
        d_out = out - heads_of(t, b, per, hd).astype(f32)
        delta = jnp.sum(d_out * out, axis=1, keepdims=True)
        d_out_b = d_out.astype(bf16)
        probs = wc * wide(inv, n_cart)
        ds = probs * (nt(d_out_b, cart_v) - delta)
        gk = gk + tn(ds.astype(bf16), qh)
        gv = gv + tn(probs.astype(bf16), d_out_b)
    whole = jnp.concatenate([gk * scale, gv], axis=1).astype(bf16)
    for j, mask in enumerate(masks):
        to = pl.multiple_of((me ^ mask) * crows, crows)
        grad[pl.ds(to, crows)] = whole[j * crows : (j + 1) * crows]


def summed(parts):
    parts = [x.astype(f32) for x in parts]
    if len(parts) == 2:
        return parts[0] + parts[1]
    own, one, two, both = parts
    return (own + both) + (one + two)


def square_kernel(*refs):
    total, squares = refs[-2:]
    g = summed([ref[...] for ref in refs[:-2]])
    total[...] = g
    squares[...] = jnp.broadcast_to(jnp.sum(g * g, keepdims=True), squares.shape)


def update(g, ma, m1, m2):
    one = beta_one * m1 + (1.0 - beta_one) * g
    two = beta_two * m2 + (1.0 - beta_two) * g * g
    return one, two, ma - learn_rate * one / (jnp.sqrt(two) + adam_eps)


def final_kernel(masks, chain, n_dp, scale, per, count, q, acc_in, total_in, top_in, g, sq_a, sq_b, st_near, st_far, ma, m1, m2, out, ma_o, m1_o, m2_o, cart):
    rows, hd = q.shape[0], acc_in.shape[1]
    group = q.shape[1] // hd
    crows, width = ma.shape[0], ma.shape[2]
    me, my_dp = lax.axis_index("ctx"), lax.axis_index("dp")
    two = scale * log2_e
    mean = (sq_a[0:1, 0:1] + sq_b[0:1, 0:1]) * (1.0 / count)
    inv_rms = 1.0 / jnp.sqrt(mean + norm_eps)
    mine = g[pl.ds(pl.multiple_of(me * crows, crows), crows)]
    own = mine[:, 0:width]
    for d in range(1, n_dp):
        own = jnp.where(my_dp == d, mine[:, d * width : (d + 1) * width], own)
    one, sec, new = update(own * inv_rms, ma[:, 0, :], m1[:, 0, :], m2[:, 0, :])
    m1_o[:, 0, :] = one
    m2_o[:, 0, :] = sec
    ma_o[:, 0, :] = new
    for r, mask in enumerate(masks):
        parts = [[], [], []]
        st = st_far if mask & chain[-1][1] else st_near
        for d in range(n_dp):
            at = (spot(chain[:-1], "ctx", mask) + spot(chain[:-1], "dp", my_dp ^ d)) * 3 * crows
            for n in range(3):
                parts[n].append(st[pl.ds(pl.multiple_of(at + n * crows, crows), crows)])
        ma_r, m1_r, m2_r = (jnp.concatenate(x, axis=1) for x in parts)
        rows_g = g[pl.ds(pl.multiple_of((me ^ mask) * crows, crows), crows)]
        _, _, new = update(rows_g * inv_rms, ma_r, m1_r, m2_r)
        cart[r * crows : (r + 1) * crows] = new.astype(bf16)
    cart_k = cart[:, :hd]
    cart_v = cart[:, hd:]
    cart_vx = jnp.concatenate([cart_v, jnp.ones_like(cart_v)], axis=1)
    span = per * rows
    for b in range(group // per):
        heads = range(b * per, (b + 1) * per)
        qh = jnp.concatenate([q[:, h * hd : (h + 1) * hd] for h in heads], axis=0)
        cut = slice(b * span, (b + 1) * span)
        top = top_in[cut]
        sc = nt(qh, cart_k) * two
        both = jnp.maximum(top, jnp.max(sc, axis=1, keepdims=True))
        wc = jnp.exp2(sc - wide(both, sc.shape[1])).astype(bf16)
        keep = jnp.exp2(top - both)
        more = nn(wc, cart_vx)
        res = ((acc_in[cut] * keep + more[:, :hd]) / (total_in[cut] * keep + more[:, hd:])).astype(bf16)
        for n, h in enumerate(heads):
            out[:, h * hd : (h + 1) * hd] = res[n * rows : (n + 1) * rows]


VMEM = pl.BlockSpec(memory_space=pltpu.VMEM)


def call(body, outs, n_in, scratch=(), limit=40):
    return pl.pallas_call(
        body,
        out_shape=outs,
        in_specs=[VMEM] * n_in,
        out_specs=tuple(VMEM for _ in outs),
        scratch_shapes=list(scratch),
        compiler_params=pltpu.CompilerParams(vmem_limit_bytes=limit * 2**20),
    )


def local(sizes, queries, targets, document_keys, document_values, doc_pos, cart_keys, cartridge_values, master, first_moment1, second_moment2):
    n_dp, n_ctx, n_head = sizes
    hd = document_keys.shape[2]
    rows = queries.shape[1]
    group = queries.shape[2] // hd
    crows = cart_keys.shape[0]
    scale = hd ** (-0.5)
    per = math.gcd(group, 4)
    steps, dp_steps, head_steps = xor_steps(n_ctx), xor_steps(n_dp), xor_steps(n_head)
    sds = jax.ShapeDtypeStruct
    stride = 2 * rows + 2 * crows + 16
    masks = [0]
    for s in steps:
        masks += [m ^ s for m in masks]
    msg, st = pl.pallas_call(
        pack_kernel,
        out_shape=(sds((stride, hd), bf16), sds((3 * crows, master.shape[2]), f32)),
        in_specs=[pl.BlockSpec(memory_space=pltpu.HBM)] * 8,
        out_specs=(VMEM, VMEM),
        scratch_shapes=[pltpu.VMEM(doc_pos.shape, jnp.int32), pltpu.SemaphoreType.DMA((8,))],
        compiler_params=pltpu.CompilerParams(vmem_limit_bytes=8 * 2**20),
    )(
        *(
            pltpu.with_memory_space_constraint(x, pltpu.HBM)
            for x in (document_keys, document_values, doc_pos, cart_keys, cartridge_values, master, first_moment1, second_moment2)
        )
    )
    q, t = queries[0], targets[0]
    cart = n_ctx * crows
    shapes = (sds((rows * group, hd), f32),) * 3
    last = steps[-1]
    held, fresh, mirrored = [msg], [msg], []
    for s in steps[:-1]:
        older = held[: len(held) - len(fresh)]
        got = [swap(joined(older), "ctx", s, n_ctx)] if older else []
        got.append(swap(joined(fresh), "ctx", s, n_ctx))
        mirrored.append(swap(joined(fresh), "ctx", last, n_ctx))
        held, fresh = held + got, got
    mirrored.append(swap(joined(fresh), "ctx", last, n_ctx))
    msgs = held + mirrored
    body = functools.partial(chunk_kernel, len(msgs) - 1, scale, per, rows, stride)
    state = call(body, shapes, 1 + len(msgs))(q, msg, *msgs[:-1])
    chain = [("ctx", s) for s in steps]
    chain[1:1] = [("dp", s) for s in dp_steps]
    for n, (axis, s) in enumerate(chain):
        if n:
            st = lax.optimization_barrier(jnp.concatenate([st, more], axis=0))
        more = swap(st, axis, s, {"ctx": n_ctx, "dp": n_dp}[axis])
    body = functools.partial(gradient_kernel, 1, masks, scale, math.gcd(group, 8), rows, stride)
    *state, grad = call(body, shapes + (sds((cart, 2 * hd), bf16),), 5 + len(msgs))(q, t, *state, *msgs)
    bits = steps + [s * n_ctx for s in dp_steps]
    rounds = [bits[n : n + 2] for n in range(0, len(bits), 2)]
    for n, pair in enumerate(rounds):
        ways = pair + [sum(pair)] if len(pair) == 2 else pair
        others = [swap(grad, ("dp", "ctx"), m, n_dp * n_ctx) for m in ways]
        if n + 1 < len(rounds):
            grad = summed([grad] + others).astype(bf16)
    total, squares = call(square_kernel, (sds((cart, 2 * hd), f32), sds((8, hd), f32)), 1 + len(others))(grad, *others)
    mine = squares
    theirs = jnp.zeros_like(squares)
    for n, s in enumerate(head_steps):
        if n:
            mine = mine + theirs
        theirs = swap(mine, "head", s, n_head)
    count = master.size * n_dp * n_ctx * n_head
    new_out, new_master, new_m1, new_m2 = call(
        functools.partial(final_kernel, masks, chain, n_dp, scale, per, count),
        (sds((rows, group * hd), bf16), sds(master.shape, f32), sds(master.shape, f32), sds(master.shape, f32)),
        12,
        [pltpu.VMEM((cart, 2 * hd), bf16)],
    )(q, *state, total, mine, theirs, st, more, master, first_moment1, second_moment2)
    return (new_out[None], new_master, new_m1, new_m2)


def solution(mesh):
    in_specs = (
        P("dp", "ctx", "head"),
        P("dp", "ctx", "head"),
        P("dp", "ctx", "head"),
        P("dp", "ctx", "head"),
        P("dp", "ctx"),
        P("ctx", "head"),
        P("ctx", "head"),
        P("ctx", "head", "dp"),
        P("ctx", "head", "dp"),
        P("ctx", "head", "dp"),
    )
    out_specs = (
        P("dp", "ctx", "head"),
        P("ctx", "head", "dp"),
        P("ctx", "head", "dp"),
        P("ctx", "head", "dp"),
    )
    sizes = (mesh.shape["dp"], mesh.shape["ctx"], mesh.shape["head"])

    def step(*args):
        return local(sizes, *args)

    return jax.shard_map(step, mesh=mesh, in_specs=in_specs, out_specs=out_specs, check_vma=False)
```

```python
import functools
import math

import jax
import jax.numpy as jnp
from jax import lax
from jax.experimental import pallas as pl
from jax.experimental.pallas import tpu as pltpu
from jax.sharding import PartitionSpec as P


beta_one = 0.8
beta_two = 0.95
learn_rate = 0.1
adam_eps = 1e-08
norm_eps = 1e-06
neg_big = -1e30
log2_e = math.log2(math.e)
pos_base = 256.0
f32, bf16 = jnp.float32, jnp.bfloat16


def xor_steps(size):
    assert size & (size - 1) == 0
    return [1 << b for b in reversed(range(size.bit_length() - 1))]


def swap(x, axis, mask, size):
    return lax.ppermute(x, axis, [(i, i ^ mask) for i in range(size)])


def joined(parts):
    return jnp.concatenate(parts, axis=0) if len(parts) > 1 else parts[0]


def spot(chain, axis, mask):
    at = 0
    for n, (name, step) in enumerate(chain):
        if name == axis:
            at = at + (((mask >> (step.bit_length() - 1)) & 1) << n)
    return at


def nt(a, b):
    return lax.dot_general(a, b, (((1,), (1,)), ((), ())), preferred_element_type=f32)


def tn(a, b):
    return lax.dot_general(a, b, (((0,), (0,)), ((), ())), preferred_element_type=f32)


def nn(a, b):
    return jnp.dot(a, b, preferred_element_type=f32)


def pack_kernel(k, v, pos, ck, cv, ma, m1, m2, msg, st, line, sems):
    rows, crows, hd = k.shape[1], ck.shape[0], k.shape[2]
    at = 2 * rows
    copies = [
        (k.at[0], msg.at[0:rows]),
        (v.at[0], msg.at[rows:at]),
        (ck, msg.at[at : at + crows]),
        (cv, msg.at[at + crows : at + 2 * crows]),
        (pos, line),
    ]
    copies += [(ref.at[:, 0, :], st.at[n * crows : (n + 1) * crows]) for n, ref in enumerate((ma, m1, m2))]
    started = [pltpu.make_async_copy(x, y, sems.at[n]) for n, (x, y) in enumerate(copies)]
    for copy in started:
        copy.start()
    for copy in started:
        copy.wait()
    at += 2 * crows
    p = line[...].astype(f32)
    hi = jnp.floor(p * (1.0 / pos_base))
    lo = p - hi * pos_base
    row = lax.broadcasted_iota(jnp.int32, (16, hd), 0)
    both = jnp.where(row == 0, jnp.broadcast_to(hi, (16, hd)), jnp.broadcast_to(lo, (16, hd)))
    msg[at : at + 16] = both.astype(bf16)


def split(refs, stride):
    return [(ref, j * stride) for ref in refs for j in range(ref.shape[0] // stride)]


def positions(ref, at, stride):
    two_rows = ref[at + stride - 16 : at + stride].astype(f32)
    return two_rows[0:1] * pos_base + two_rows[1:2]


def document_part(own, blocks, rows, stride):
    query_pos = jnp.broadcast_to(positions(own, 0, stride), (rows, rows))
    keys, values = [], []
    for ref, at in blocks:
        key_pos = jnp.broadcast_to(positions(ref, at, stride), (rows, rows)).T
        barred = jnp.where(key_pos <= query_pos, 0.0, neg_big).astype(bf16)
        keys.append(jnp.concatenate([ref[at : at + rows], barred], axis=1))
        values.append(ref[at + rows : at + 2 * rows])
    values = jnp.concatenate(values, axis=0)
    return jnp.concatenate(keys, axis=0), jnp.concatenate([values, jnp.ones_like(values)], axis=1)


def heads_of(ref, b, per, hd):
    return jnp.concatenate([ref[:, h * hd : (h + 1) * hd] for h in range(b * per, (b + 1) * per)], axis=0)


def pick(rows, per):
    line = lax.broadcasted_iota(jnp.int32, (rows, rows), 0)
    lane = lax.broadcasted_iota(jnp.int32, (rows, rows), 1)
    one = jnp.where(line == lane, 1.0, 0.0).astype(bf16)
    return jnp.concatenate([one] * per, axis=0)


def wide(x, columns):
    return jnp.concatenate([x] * (columns // x.shape[1]), axis=1)


def attend(qx, part, two, state):
    keys, values = part
    s = nt(qx, keys) * two
    top = jnp.max(s, axis=1, keepdims=True)
    hd = values.shape[1] // 2
    if state is None:
        top = jnp.broadcast_to(top, (s.shape[0], hd))
        both = nn(jnp.exp2(s - wide(top, s.shape[1])).astype(bf16), values)
        return both[:, :hd], both[:, hd:], top
    acc, total, old = state
    top = jnp.maximum(old, top)
    both = nn(jnp.exp2(s - wide(top, s.shape[1])).astype(bf16), values)
    keep = jnp.exp2(old - top)
    return acc * keep + both[:, :hd], total * keep + both[:, hd:], top


def chunk_kernel(n_msgs, scale, per, rows, stride, *refs):
    q, own, msgs = refs[0], refs[1], refs[2 : 2 + n_msgs]
    outs = refs[2 + n_msgs :]
    hd = own.shape[1]
    part = document_part(own, split(msgs, stride), rows, stride)
    eye = pick(rows, per)
    span = per * rows
    for b in range(q.shape[1] // hd // per):
        cut = slice(b * span, (b + 1) * span)
        qx = jnp.concatenate([heads_of(q, b, per, hd), eye], axis=1)
        for ref, x in zip(outs, attend(qx, part, scale * log2_e, None)):
            ref[cut] = x


def gradient_kernel(n_last, masks, scale, per, rows, stride, *refs):
    q, t = refs[:2]
    olds = refs[2:5]
    outs, grad = refs[-4:-1], refs[-1]
    msgs = refs[5:-4]
    own = msgs[0]
    hd = own.shape[1]
    crows = (stride - 2 * rows - 16) // 2
    me = lax.axis_index("ctx")
    two = scale * log2_e
    part = document_part(own, split(msgs[len(msgs) - n_last :], stride), rows, stride)
    every = [(ref, at + 2 * rows) for ref, at in split(msgs, stride)]
    cart_k = jnp.concatenate([ref[at : at + crows] for ref, at in every], axis=0)
    cart_v = jnp.concatenate([ref[at + crows : at + 2 * crows] for ref, at in every], axis=0)
    cart_vx = jnp.concatenate([cart_v, jnp.ones_like(cart_v)], axis=1)
    n_cart = cart_k.shape[0]
    eye = pick(rows, per)
    span = per * rows
    gk = jnp.zeros((n_cart, hd), f32)
    gv = jnp.zeros((n_cart, hd), f32)
    for b in range(q.shape[1] // hd // per):
        cut = slice(b * span, (b + 1) * span)
        qh = heads_of(q, b, per, hd)
        acc, total, top = attend(jnp.concatenate([qh, eye], axis=1), part, two, tuple(ref[cut] for ref in olds))
        for ref, x in zip(outs, (acc, total, top)):
            ref[cut] = x
        sc = nt(qh, cart_k) * two
        both = jnp.maximum(top, jnp.max(sc, axis=1, keepdims=True))
        wc = jnp.exp2(sc - wide(both, n_cart))
        keep = jnp.exp2(top - both)
        more = nn(wc.astype(bf16), cart_vx)
        inv = 1.0 / (total * keep + more[:, hd:])
        out = (acc * keep + more[:, :hd]) * inv
        d_out = out - heads_of(t, b, per, hd).astype(f32)
        delta = jnp.sum(d_out * out, axis=1, keepdims=True)
        d_out_b = d_out.astype(bf16)
        probs = wc * wide(inv, n_cart)
        ds = probs * (nt(d_out_b, cart_v) - delta)
        gk = gk + tn(ds.astype(bf16), qh)
        gv = gv + tn(probs.astype(bf16), d_out_b)
    whole = jnp.concatenate([gk * scale, gv], axis=1).astype(bf16)
    for j, mask in enumerate(masks):
        to = pl.multiple_of((me ^ mask) * crows, crows)
        grad[pl.ds(to, crows)] = whole[j * crows : (j + 1) * crows]


def summed(parts):
    parts = [x.astype(f32) for x in parts]
    if len(parts) == 2:
        return parts[0] + parts[1]
    own, one, two, both = parts
    return (own + both) + (one + two)


def square_kernel(*refs):
    total, squares = refs[-2:]
    g = summed([ref[...] for ref in refs[:-2]])
    total[...] = g
    squares[...] = jnp.broadcast_to(jnp.sum(g * g, keepdims=True), squares.shape)


def update(g, ma, m1, m2):
    one = beta_one * m1 + (1.0 - beta_one) * g
    two = beta_two * m2 + (1.0 - beta_two) * g * g
    return one, two, ma - learn_rate * one / (jnp.sqrt(two) + adam_eps)


def final_kernel(masks, chain, n_dp, scale, per, count, q, acc_in, total_in, top_in, g, sq_a, sq_b, st_near, st_far, *rest):
    rows, hd = q.shape[0], acc_in.shape[1]
    group = q.shape[1] // hd
    crows, width = rest[1].shape[0], rest[1].shape[2]
    me, my_dp = lax.axis_index("ctx"), lax.axis_index("dp")
    two = scale * log2_e
    out_hbm, small_hbm = rest[0], rest[1:4]
    out, small, cart, sems = rest[4], rest[5:8], rest[8], rest[9]
    copies = []

    def send(source, target):
        copies.append(pltpu.make_async_copy(source, target, sems.at[len(copies)]))
        copies[-1].start()

    mean = (sq_a[0:1, 0:1] + sq_b[0:1, 0:1]) * (1.0 / count)
    inv_rms = 1.0 / jnp.sqrt(mean + norm_eps)
    mine = g[pl.ds(pl.multiple_of(me * crows, crows), crows)]
    own = mine[:, 0:width]
    for d in range(1, n_dp):
        own = jnp.where(my_dp == d, mine[:, d * width : (d + 1) * width], own)
    one, sec, new = update(own * inv_rms, *(st_near[n * crows : (n + 1) * crows] for n in range(3)))
    for ref, target, x in zip(small, small_hbm, (new, one, sec)):
        ref[:, 0, :] = x
        send(ref, target)
    for r, mask in enumerate(masks):
        parts = [[], [], []]
        st = st_far if mask & chain[-1][1] else st_near
        for d in range(n_dp):
            at = (spot(chain[:-1], "ctx", mask) + spot(chain[:-1], "dp", my_dp ^ d)) * 3 * crows
            for n in range(3):
                parts[n].append(st[pl.ds(pl.multiple_of(at + n * crows, crows), crows)])
        ma_r, m1_r, m2_r = (jnp.concatenate(x, axis=1) for x in parts)
        rows_g = g[pl.ds(pl.multiple_of((me ^ mask) * crows, crows), crows)]
        _, _, new = update(rows_g * inv_rms, ma_r, m1_r, m2_r)
        cart[r * crows : (r + 1) * crows] = new.astype(bf16)
    cart_k = cart[:, :hd]
    cart_v = cart[:, hd:]
    cart_vx = jnp.concatenate([cart_v, jnp.ones_like(cart_v)], axis=1)
    span = per * rows
    for b in range(group // per):
        heads = range(b * per, (b + 1) * per)
        qh = jnp.concatenate([q[:, h * hd : (h + 1) * hd] for h in heads], axis=0)
        cut = slice(b * span, (b + 1) * span)
        top = top_in[cut]
        sc = nt(qh, cart_k) * two
        both = jnp.maximum(top, jnp.max(sc, axis=1, keepdims=True))
        wc = jnp.exp2(sc - wide(both, sc.shape[1])).astype(bf16)
        keep = jnp.exp2(top - both)
        more = nn(wc, cart_vx)
        res = ((acc_in[cut] * keep + more[:, :hd]) / (total_in[cut] * keep + more[:, hd:])).astype(bf16)
        for n, h in enumerate(heads):
            out[:, h * hd : (h + 1) * hd] = res[n * rows : (n + 1) * rows]
        columns = slice(b * per * hd, (b + 1) * per * hd)
        send(out.at[:, columns], out_hbm.at[:, columns])
    for copy in copies:
        copy.wait()


VMEM = pl.BlockSpec(memory_space=pltpu.VMEM)


def call(body, outs, n_in, scratch=(), limit=40, space=VMEM):
    return pl.pallas_call(
        body,
        out_shape=outs,
        in_specs=[VMEM] * n_in,
        out_specs=tuple(space for _ in outs),
        scratch_shapes=list(scratch),
        compiler_params=pltpu.CompilerParams(vmem_limit_bytes=limit * 2**20),
    )


def local(sizes, queries, targets, document_keys, document_values, doc_pos, cart_keys, cartridge_values, master, first_moment1, second_moment2):
    n_dp, n_ctx, n_head = sizes
    hd = document_keys.shape[2]
    rows = queries.shape[1]
    group = queries.shape[2] // hd
    crows = cart_keys.shape[0]
    scale = hd ** (-0.5)
    steps, dp_steps, head_steps = xor_steps(n_ctx), xor_steps(n_dp), xor_steps(n_head)
    sds = jax.ShapeDtypeStruct
    stride = 2 * rows + 2 * crows + 16
    masks = [0]
    for s in steps:
        masks += [m ^ s for m in masks]
    msg, st = pl.pallas_call(
        pack_kernel,
        out_shape=(sds((stride, hd), bf16), sds((3 * crows, master.shape[2]), f32)),
        in_specs=[pl.BlockSpec(memory_space=pltpu.HBM)] * 8,
        out_specs=(VMEM, VMEM),
        scratch_shapes=[pltpu.VMEM(doc_pos.shape, jnp.int32), pltpu.SemaphoreType.DMA((8,))],
        compiler_params=pltpu.CompilerParams(vmem_limit_bytes=8 * 2**20),
    )(
        *(
            pltpu.with_memory_space_constraint(x, pltpu.HBM)
            for x in (document_keys, document_values, doc_pos, cart_keys, cartridge_values, master, first_moment1, second_moment2)
        )
    )
    q, t = queries[0], targets[0]
    cart = n_ctx * crows
    shapes = (sds((rows * group, hd), f32),) * 3
    last = steps[-1]
    held, fresh, mirrored = [msg], [msg], []
    for s in steps[:-1]:
        older = held[: len(held) - len(fresh)]
        got = [swap(joined(older), "ctx", s, n_ctx)] if older else []
        got.append(swap(joined(fresh), "ctx", s, n_ctx))
        mirrored.append(swap(joined(fresh), "ctx", last, n_ctx))
        held, fresh = held + got, got
    mirrored.append(swap(joined(fresh), "ctx", last, n_ctx))
    msgs = held + mirrored
    body = functools.partial(chunk_kernel, len(msgs) - 1, scale, math.gcd(group, 2), rows, stride)
    state = call(body, shapes, 1 + len(msgs))(q, msg, *msgs[:-1])
    chain = [("ctx", s) for s in steps]
    chain[1:1] = [("dp", s) for s in dp_steps]
    for n, (axis, s) in enumerate(chain):
        if n:
            st = lax.optimization_barrier(jnp.concatenate([st, more], axis=0))
        more = swap(st, axis, s, {"ctx": n_ctx, "dp": n_dp}[axis])
    body = functools.partial(gradient_kernel, 1, masks, scale, math.gcd(group, 16), rows, stride)
    *state, grad = call(body, shapes + (sds((cart, 2 * hd), bf16),), 5 + len(msgs))(q, t, *state, *msgs)
    bits = steps + [s * n_ctx for s in dp_steps]
    rounds = [bits[n : n + 2] for n in range(0, len(bits), 2)]
    for n, pair in enumerate(rounds):
        ways = pair + [sum(pair)] if len(pair) == 2 else pair
        others = [swap(grad, ("dp", "ctx"), m, n_dp * n_ctx) for m in ways]
        if n + 1 < len(rounds):
            grad = summed([grad] + others).astype(bf16)
    total, squares = call(square_kernel, (sds((cart, 2 * hd), f32), sds((8, hd), f32)), 1 + len(others))(grad, *others)
    mine = squares
    theirs = jnp.zeros_like(squares)
    for n, s in enumerate(head_steps):
        if n:
            mine = mine + theirs
        theirs = swap(mine, "head", s, n_head)
    count = master.size * n_dp * n_ctx * n_head
    new_out, new_master, new_m1, new_m2 = call(
        functools.partial(final_kernel, masks, chain, n_dp, scale, math.gcd(group, 8), count),
        (sds((rows, group * hd), bf16),) + (sds(master.shape, f32),) * 3,
        9,
        [pltpu.VMEM((rows, group * hd), bf16)]
        + [pltpu.VMEM(master.shape, f32)] * 3
        + [pltpu.VMEM((cart, 2 * hd), bf16), pltpu.SemaphoreType.DMA((3 + group,))],
        space=pl.BlockSpec(memory_space=pltpu.HBM),
    )(q, *state, total, mine, theirs, st, more)
    return (new_out[None], new_master, new_m1, new_m2)


def solution(mesh):
    in_specs = (
        P("dp", "ctx", "head"),
        P("dp", "ctx", "head"),
        P("dp", "ctx", "head"),
        P("dp", "ctx", "head"),
        P("dp", "ctx"),
        P("ctx", "head"),
        P("ctx", "head"),
        P("ctx", "head", "dp"),
        P("ctx", "head", "dp"),
        P("ctx", "head", "dp"),
    )
    out_specs = (
        P("dp", "ctx", "head"),
        P("ctx", "head", "dp"),
        P("ctx", "head", "dp"),
        P("ctx", "head", "dp"),
    )
    sizes = (mesh.shape["dp"], mesh.shape["ctx"], mesh.shape["head"])

    def step(*args):
        return local(sizes, *args)

    return jax.shard_map(step, mesh=mesh, in_specs=in_specs, out_specs=out_specs, check_vma=False)
```

```python
import functools
import math

import jax
import jax.numpy as jnp
from jax import lax
from jax.experimental import pallas as pl
from jax.experimental.pallas import tpu as pltpu
from jax.sharding import PartitionSpec as P


beta_one = 0.8
beta_two = 0.95
learn_rate = 0.1
adam_eps = 1e-08
norm_eps = 1e-06
neg_big = -1e30
log2_e = math.log2(math.e)
pos_base = 256.0
f32, bf16 = jnp.float32, jnp.bfloat16


def xor_steps(size):
    assert size & (size - 1) == 0
    return [1 << b for b in reversed(range(size.bit_length() - 1))]


def swap(x, axis, mask, size):
    return lax.ppermute(x, axis, [(i, i ^ mask) for i in range(size)])


def joined(parts):
    return jnp.concatenate(parts, axis=0) if len(parts) > 1 else parts[0]


def spot(chain, axis, mask):
    at = 0
    for n, (name, step) in enumerate(chain):
        if name == axis:
            at = at + (((mask >> (step.bit_length() - 1)) & 1) << n)
    return at


def nt(a, b):
    return lax.dot_general(a, b, (((1,), (1,)), ((), ())), preferred_element_type=f32)


def tn(a, b):
    return lax.dot_general(a, b, (((0,), (0,)), ((), ())), preferred_element_type=f32)


def nn(a, b):
    return jnp.dot(a, b, preferred_element_type=f32)


def pack_kernel(k, v, pos, ck, cv, ma, m1, m2, q, msg, st, q_here, line, sems):
    rows, crows, hd = k.shape[1], ck.shape[0], k.shape[2]
    at = 2 * rows
    copies = [
        (k.at[0], msg.at[0:rows]),
        (v.at[0], msg.at[rows:at]),
        (ck, msg.at[at : at + crows]),
        (cv, msg.at[at + crows : at + 2 * crows]),
        (pos, line),
    ]
    copies += [(ref.at[:, 0, :], st.at[n * crows : (n + 1) * crows]) for n, ref in enumerate((ma, m1, m2))]
    copies.append((q.at[0], q_here))
    started = [pltpu.make_async_copy(x, y, sems.at[n]) for n, (x, y) in enumerate(copies)]
    for copy in started:
        copy.start()
    for copy in started:
        copy.wait()
    at += 2 * crows
    p = line[...].astype(f32)
    hi = jnp.floor(p * (1.0 / pos_base))
    lo = p - hi * pos_base
    row = lax.broadcasted_iota(jnp.int32, (16, hd), 0)
    both = jnp.where(row == 0, jnp.broadcast_to(hi, (16, hd)), jnp.broadcast_to(lo, (16, hd)))
    msg[at : at + 16] = both.astype(bf16)


def split(refs, stride):
    return [(ref, j * stride) for ref in refs for j in range(ref.shape[0] // stride)]


def positions(ref, at, stride):
    two_rows = ref[at + stride - 16 : at + stride].astype(f32)
    return two_rows[0:1] * pos_base + two_rows[1:2]


def document_part(own, blocks, rows, stride):
    query_pos = jnp.broadcast_to(positions(own, 0, stride), (rows, rows))
    keys, values = [], []
    for ref, at in blocks:
        key_pos = jnp.broadcast_to(positions(ref, at, stride), (rows, rows)).T
        barred = jnp.where(key_pos <= query_pos, 0.0, neg_big).astype(bf16)
        keys.append(jnp.concatenate([ref[at : at + rows], barred], axis=1))
        values.append(ref[at + rows : at + 2 * rows])
    values = jnp.concatenate(values, axis=0)
    return jnp.concatenate(keys, axis=0), jnp.concatenate([values, jnp.ones_like(values)], axis=1)


def heads_of(ref, b, per, hd):
    return jnp.concatenate([ref[:, h * hd : (h + 1) * hd] for h in range(b * per, (b + 1) * per)], axis=0)


def pick(rows, per):
    line = lax.broadcasted_iota(jnp.int32, (rows, rows), 0)
    lane = lax.broadcasted_iota(jnp.int32, (rows, rows), 1)
    one = jnp.where(line == lane, 1.0, 0.0).astype(bf16)
    return jnp.concatenate([one] * per, axis=0)


def wide(x, columns):
    return jnp.concatenate([x] * (columns // x.shape[1]), axis=1)


def attend(qx, part, two, state):
    keys, values = part
    s = nt(qx, keys) * two
    top = jnp.max(s, axis=1, keepdims=True)
    hd = values.shape[1] // 2
    if state is None:
        top = jnp.broadcast_to(top, (s.shape[0], hd))
        both = nn(jnp.exp2(s - wide(top, s.shape[1])).astype(bf16), values)
        return both[:, :hd], both[:, hd:], top
    acc, total, old = state
    top = jnp.maximum(old, top)
    both = nn(jnp.exp2(s - wide(top, s.shape[1])).astype(bf16), values)
    keep = jnp.exp2(old - top)
    return acc * keep + both[:, :hd], total * keep + both[:, hd:], top


def chunk_kernel(skipped, n_msgs, scale, per, rows, stride, *refs):
    q, own, msgs = refs[0], refs[1], refs[2 : 2 + n_msgs]
    olds, outs = refs[2 + n_msgs : -3], refs[-3:]
    hd = own.shape[1]
    blocks = split(msgs, stride)
    part = document_part(own, blocks[: len(blocks) - skipped], rows, stride)
    eye = pick(rows, per)
    span = per * rows
    for b in range(q.shape[1] // hd // per):
        cut = slice(b * span, (b + 1) * span)
        qx = jnp.concatenate([heads_of(q, b, per, hd), eye], axis=1)
        state = tuple(ref[cut] for ref in olds) if olds else None
        for ref, x in zip(outs, attend(qx, part, scale * log2_e, state)):
            ref[cut] = x


def gradient_kernel(first_blocks, masks, scale, per, rows, stride, *refs):
    q, t = refs[:2]
    olds = refs[2:5]
    outs, grad = refs[-4:-1], refs[-1]
    msgs = refs[5:-4]
    own = msgs[0]
    hd = own.shape[1]
    crows = (stride - 2 * rows - 16) // 2
    me = lax.axis_index("ctx")
    two = scale * log2_e
    part = document_part(own, split(msgs, stride)[first_blocks:], rows, stride)
    every = [(ref, at + 2 * rows) for ref, at in split(msgs, stride)]
    cart_k = jnp.concatenate([ref[at : at + crows] for ref, at in every], axis=0)
    cart_v = jnp.concatenate([ref[at + crows : at + 2 * crows] for ref, at in every], axis=0)
    cart_vx = jnp.concatenate([cart_v, jnp.ones_like(cart_v)], axis=1)
    n_cart = cart_k.shape[0]
    eye = pick(rows, per)
    span = per * rows
    gk = jnp.zeros((n_cart, hd), f32)
    gv = jnp.zeros((n_cart, hd), f32)
    for b in range(q.shape[1] // hd // per):
        cut = slice(b * span, (b + 1) * span)
        qh = heads_of(q, b, per, hd)
        acc, total, top = attend(jnp.concatenate([qh, eye], axis=1), part, two, tuple(ref[cut] for ref in olds))
        for ref, x in zip(outs, (acc, total, top)):
            ref[cut] = x
        sc = nt(qh, cart_k) * two
        both = jnp.maximum(top, jnp.max(sc, axis=1, keepdims=True))
        wc = jnp.exp2(sc - wide(both, n_cart))
        keep = jnp.exp2(top - both)
        more = nn(wc.astype(bf16), cart_vx)
        inv = 1.0 / (total * keep + more[:, hd:])
        out = (acc * keep + more[:, :hd]) * inv
        d_out = out - heads_of(t, b, per, hd).astype(f32)
        delta = jnp.sum(d_out * out, axis=1, keepdims=True)
        d_out_b = d_out.astype(bf16)
        probs = wc * wide(inv, n_cart)
        ds = probs * (nt(d_out_b, cart_v) - delta)
        gk = gk + tn(ds.astype(bf16), qh)
        gv = gv + tn(probs.astype(bf16), d_out_b)
    whole = jnp.concatenate([gk * scale, gv], axis=1).astype(bf16)
    for j, mask in enumerate(masks):
        to = pl.multiple_of((me ^ mask) * crows, crows)
        grad[pl.ds(to, crows)] = whole[j * crows : (j + 1) * crows]


def summed(parts):
    parts = [x.astype(f32) for x in parts]
    if len(parts) == 2:
        return parts[0] + parts[1]
    own, one, two, both = parts
    return (own + both) + (one + two)


def square_kernel(*refs):
    total, squares = refs[-2:]
    g = summed([ref[...] for ref in refs[:-2]])
    total[...] = g
    squares[...] = jnp.broadcast_to(jnp.sum(g * g, keepdims=True), squares.shape)


def update(g, ma, m1, m2):
    one = beta_one * m1 + (1.0 - beta_one) * g
    two = beta_two * m2 + (1.0 - beta_two) * g * g
    return one, two, ma - learn_rate * one / (jnp.sqrt(two) + adam_eps)


def final_kernel(masks, chain, n_dp, scale, per, count, q, acc_in, total_in, top_in, g, sq_a, sq_b, st_near, st_far, *rest):
    rows, hd = q.shape[0], acc_in.shape[1]
    group = q.shape[1] // hd
    crows, width = rest[1].shape[0], rest[1].shape[2]
    me, my_dp = lax.axis_index("ctx"), lax.axis_index("dp")
    two = scale * log2_e
    out_hbm, small_hbm = rest[0], rest[1:4]
    out, small, cart, sems = rest[4], rest[5:8], rest[8], rest[9]
    copies = []

    def send(source, target):
        copies.append(pltpu.make_async_copy(source, target, sems.at[len(copies)]))
        copies[-1].start()

    mean = (sq_a[0:1, 0:1] + sq_b[0:1, 0:1]) * (1.0 / count)
    inv_rms = 1.0 / jnp.sqrt(mean + norm_eps)
    mine = g[pl.ds(pl.multiple_of(me * crows, crows), crows)]
    own = mine[:, 0:width]
    for d in range(1, n_dp):
        own = jnp.where(my_dp == d, mine[:, d * width : (d + 1) * width], own)
    one, sec, new = update(own * inv_rms, *(st_near[n * crows : (n + 1) * crows] for n in range(3)))
    for ref, target, x in zip(small, small_hbm, (new, one, sec)):
        ref[:, 0, :] = x
        send(ref, target)
    for r, mask in enumerate(masks):
        parts = [[], [], []]
        st = st_far if mask & chain[-1][1] else st_near
        for d in range(n_dp):
            at = (spot(chain[:-1], "ctx", mask) + spot(chain[:-1], "dp", my_dp ^ d)) * 3 * crows
            for n in range(3):
                parts[n].append(st[pl.ds(pl.multiple_of(at + n * crows, crows), crows)])
        ma_r, m1_r, m2_r = (jnp.concatenate(x, axis=1) for x in parts)
        rows_g = g[pl.ds(pl.multiple_of((me ^ mask) * crows, crows), crows)]
        _, _, new = update(rows_g * inv_rms, ma_r, m1_r, m2_r)
        cart[r * crows : (r + 1) * crows] = new.astype(bf16)
    cart_k = cart[:, :hd]
    cart_v = cart[:, hd:]
    cart_vx = jnp.concatenate([cart_v, jnp.ones_like(cart_v)], axis=1)
    span = per * rows
    for b in range(group // per):
        heads = range(b * per, (b + 1) * per)
        qh = jnp.concatenate([q[:, h * hd : (h + 1) * hd] for h in heads], axis=0)
        cut = slice(b * span, (b + 1) * span)
        top = top_in[cut]
        sc = nt(qh, cart_k) * two
        both = jnp.maximum(top, jnp.max(sc, axis=1, keepdims=True))
        wc = jnp.exp2(sc - wide(both, sc.shape[1])).astype(bf16)
        keep = jnp.exp2(top - both)
        more = nn(wc, cart_vx)
        res = ((acc_in[cut] * keep + more[:, :hd]) / (total_in[cut] * keep + more[:, hd:])).astype(bf16)
        for n, h in enumerate(heads):
            out[:, h * hd : (h + 1) * hd] = res[n * rows : (n + 1) * rows]
        columns = slice(b * per * hd, (b + 1) * per * hd)
        send(out.at[:, columns], out_hbm.at[:, columns])
    for copy in copies:
        copy.wait()


VMEM = pl.BlockSpec(memory_space=pltpu.VMEM)


def call(body, outs, n_in, scratch=(), limit=40, space=VMEM):
    return pl.pallas_call(
        body,
        out_shape=outs,
        in_specs=[VMEM] * n_in,
        out_specs=tuple(space for _ in outs),
        scratch_shapes=list(scratch),
        compiler_params=pltpu.CompilerParams(vmem_limit_bytes=limit * 2**20),
    )


def local(sizes, queries, targets, document_keys, document_values, doc_pos, cart_keys, cartridge_values, master, first_moment1, second_moment2):
    n_dp, n_ctx, n_head = sizes
    hd = document_keys.shape[2]
    rows = queries.shape[1]
    group = queries.shape[2] // hd
    crows = cart_keys.shape[0]
    scale = hd ** (-0.5)
    steps, dp_steps, head_steps = xor_steps(n_ctx), xor_steps(n_dp), xor_steps(n_head)
    sds = jax.ShapeDtypeStruct
    stride = 2 * rows + 2 * crows + 16
    masks = [0]
    for s in steps:
        masks += [m ^ s for m in masks]
    msg, st, q = pl.pallas_call(
        pack_kernel,
        out_shape=(sds((stride, hd), bf16), sds((3 * crows, master.shape[2]), f32), sds(queries.shape[1:], queries.dtype)),
        in_specs=[pl.BlockSpec(memory_space=pltpu.HBM)] * 9,
        out_specs=(VMEM, VMEM, VMEM),
        scratch_shapes=[pltpu.VMEM(doc_pos.shape, jnp.int32), pltpu.SemaphoreType.DMA((9,))],
        compiler_params=pltpu.CompilerParams(vmem_limit_bytes=8 * 2**20),
    )(
        *(
            pltpu.with_memory_space_constraint(x, pltpu.HBM)
            for x in (document_keys, document_values, doc_pos, cart_keys, cartridge_values, master, first_moment1, second_moment2, queries)
        )
    )
    t = targets[0]
    cart = n_ctx * crows
    shapes = (sds((rows * group, hd), f32),) * 3
    last = steps[-1]
    held, fresh, unsent, mirrored = [msg], [msg], [msg], []
    for s in steps[:-1]:
        older = held[: len(held) - len(fresh)]
        early = [swap(joined(older), "ctx", s, n_ctx)] if older else []
        newest = [swap(joined(fresh), "ctx", s, n_ctx)]
        mirrored.append(swap(joined(unsent + early), "ctx", last, n_ctx))
        fresh, unsent = early + newest, newest
        held = held + fresh
    mirrored.append(swap(joined(unsent), "ctx", last, n_ctx))
    msgs = held + mirrored
    tail = mirrored[-1].shape[0] // stride
    left = max(2, tail)

    def document(some, skipped, state):
        body = functools.partial(chunk_kernel, skipped, len(some), scale, math.gcd(group, 2), rows, stride)
        return call(body, shapes, 2 + len(some) + len(state))(q, msg, *some, *state)

    state = document(held[:-1] + mirrored[:-2], 0, ())
    state = document(held[-1:] + mirrored[-2:-1], left - tail, state)
    chain = [("ctx", s) for s in steps]
    chain[1:1] = [("dp", s) for s in dp_steps]
    for n, (axis, s) in enumerate(chain):
        if n:
            st = lax.optimization_barrier(jnp.concatenate([st, more], axis=0))
        more = swap(st, axis, s, {"ctx": n_ctx, "dp": n_dp}[axis])
    body = functools.partial(gradient_kernel, n_ctx - left, masks, scale, math.gcd(group, 16), rows, stride)
    *state, grad = call(body, shapes + (sds((cart, 2 * hd), bf16),), 5 + len(msgs))(q, t, *state, *msgs)
    bits = steps + [s * n_ctx for s in dp_steps]
    rounds = [bits[n : n + 2] for n in range(0, len(bits), 2)]
    for n, pair in enumerate(rounds):
        ways = pair + [sum(pair)] if len(pair) == 2 else pair
        others = [swap(grad, ("dp", "ctx"), m, n_dp * n_ctx) for m in ways]
        if n + 1 < len(rounds):
            grad = summed([grad] + others).astype(bf16)
    total, squares = call(square_kernel, (sds((cart, 2 * hd), f32), sds((8, hd), f32)), 1 + len(others))(grad, *others)
    mine = squares
    theirs = jnp.zeros_like(squares)
    for n, s in enumerate(head_steps):
        if n:
            mine = mine + theirs
        theirs = swap(mine, "head", s, n_head)
    count = master.size * n_dp * n_ctx * n_head
    new_out, new_master, new_m1, new_m2 = call(
        functools.partial(final_kernel, masks, chain, n_dp, scale, math.gcd(group, 8), count),
        (sds((rows, group * hd), bf16),) + (sds(master.shape, f32),) * 3,
        9,
        [pltpu.VMEM((rows, group * hd), bf16)]
        + [pltpu.VMEM(master.shape, f32)] * 3
        + [pltpu.VMEM((cart, 2 * hd), bf16), pltpu.SemaphoreType.DMA((3 + group,))],
        space=pl.BlockSpec(memory_space=pltpu.HBM),
    )(q, *state, total, mine, theirs, st, more)
    return (new_out[None], new_master, new_m1, new_m2)


def solution(mesh):
    in_specs = (
        P("dp", "ctx", "head"),
        P("dp", "ctx", "head"),
        P("dp", "ctx", "head"),
        P("dp", "ctx", "head"),
        P("dp", "ctx"),
        P("ctx", "head"),
        P("ctx", "head"),
        P("ctx", "head", "dp"),
        P("ctx", "head", "dp"),
        P("ctx", "head", "dp"),
    )
    out_specs = (
        P("dp", "ctx", "head"),
        P("ctx", "head", "dp"),
        P("ctx", "head", "dp"),
        P("ctx", "head", "dp"),
    )
    sizes = (mesh.shape["dp"], mesh.shape["ctx"], mesh.shape["head"])

    def step(*args):
        return local(sizes, *args)

    return jax.shard_map(step, mesh=mesh, in_specs=in_specs, out_specs=out_specs, check_vma=False)
```

```python
import functools
import math

import jax
import jax.numpy as jnp
from jax import lax
from jax.experimental import pallas as pl
from jax.experimental.pallas import tpu as pltpu
from jax.sharding import PartitionSpec as P


beta_one = 0.8
beta_two = 0.95
learn_rate = 0.1
adam_eps = 1e-08
norm_eps = 1e-06
neg_big = -1e30
log2_e = math.log2(math.e)
pos_base = 256.0
f32, bf16 = jnp.float32, jnp.bfloat16


def xor_steps(size):
    assert size & (size - 1) == 0
    return [1 << b for b in reversed(range(size.bit_length() - 1))]


def swap(x, axis, mask, size):
    return lax.ppermute(x, axis, [(i, i ^ mask) for i in range(size)])


def joined(parts):
    return jnp.concatenate(parts, axis=0) if len(parts) > 1 else parts[0]


def spot(chain, axis, mask):
    at = 0
    for n, (name, step) in enumerate(chain):
        if name == axis:
            at = at + (((mask >> (step.bit_length() - 1)) & 1) << n)
    return at


def nt(a, b):
    return lax.dot_general(a, b, (((1,), (1,)), ((), ())), preferred_element_type=f32)


def tn(a, b):
    return lax.dot_general(a, b, (((0,), (0,)), ((), ())), preferred_element_type=f32)


def nn(a, b):
    return jnp.dot(a, b, preferred_element_type=f32)


def pack_kernel(k, v, pos, ck, cv, ma, m1, m2, msg, st, line, sems):
    rows, crows, hd = k.shape[1], ck.shape[0], k.shape[2]
    at = 2 * rows
    copies = [
        (k.at[0], msg.at[0:rows]),
        (v.at[0], msg.at[rows:at]),
        (ck, msg.at[at : at + crows]),
        (cv, msg.at[at + crows : at + 2 * crows]),
        (pos, line),
    ]
    copies += [(ref.at[:, 0, :], st.at[n * crows : (n + 1) * crows]) for n, ref in enumerate((ma, m1, m2))]
    started = [pltpu.make_async_copy(x, y, sems.at[n]) for n, (x, y) in enumerate(copies)]
    for copy in started:
        copy.start()
    for copy in started:
        copy.wait()
    at += 2 * crows
    p = line[...].astype(f32)
    hi = jnp.floor(p * (1.0 / pos_base))
    lo = p - hi * pos_base
    row = lax.broadcasted_iota(jnp.int32, (16, hd), 0)
    both = jnp.where(row == 0, jnp.broadcast_to(hi, (16, hd)), jnp.broadcast_to(lo, (16, hd)))
    msg[at : at + 16] = both.astype(bf16)


def fetch_kernel(source, target, sem):
    copy = pltpu.make_async_copy(source, target, sem)
    copy.start()
    copy.wait()


def split(refs, stride):
    return [(ref, j * stride) for ref in refs for j in range(ref.shape[0] // stride)]


def positions(ref, at, stride):
    two_rows = ref[at + stride - 16 : at + stride].astype(f32)
    return two_rows[0:1] * pos_base + two_rows[1:2]


def document_part(own, blocks, rows, stride):
    query_pos = jnp.broadcast_to(positions(own, 0, stride), (rows, rows))
    keys, values = [], []
    for ref, at in blocks:
        key_pos = jnp.broadcast_to(positions(ref, at, stride), (rows, rows)).T
        barred = jnp.where(key_pos <= query_pos, 0.0, neg_big).astype(bf16)
        keys.append(jnp.concatenate([ref[at : at + rows], barred], axis=1))
        values.append(ref[at + rows : at + 2 * rows])
    values = jnp.concatenate(values, axis=0)
    return jnp.concatenate(keys, axis=0), jnp.concatenate([values, jnp.ones_like(values)], axis=1)


def heads_of(ref, b, per, hd):
    return jnp.concatenate([ref[:, h * hd : (h + 1) * hd] for h in range(b * per, (b + 1) * per)], axis=0)


def pick(rows, per):
    line = lax.broadcasted_iota(jnp.int32, (rows, rows), 0)
    lane = lax.broadcasted_iota(jnp.int32, (rows, rows), 1)
    one = jnp.where(line == lane, 1.0, 0.0).astype(bf16)
    return jnp.concatenate([one] * per, axis=0)


def wide(x, columns):
    return jnp.concatenate([x] * (columns // x.shape[1]), axis=1)


def attend(qx, part, two, state):
    keys, values = part
    s = nt(qx, keys) * two
    top = jnp.max(s, axis=1, keepdims=True)
    hd = values.shape[1] // 2
    if state is None:
        top = jnp.broadcast_to(top, (s.shape[0], hd))
        both = nn(jnp.exp2(s - wide(top, s.shape[1])).astype(bf16), values)
        return both[:, :hd], both[:, hd:], top
    acc, total, old = state
    top = jnp.maximum(old, top)
    both = nn(jnp.exp2(s - wide(top, s.shape[1])).astype(bf16), values)
    keep = jnp.exp2(old - top)
    return acc * keep + both[:, :hd], total * keep + both[:, hd:], top


def chunk_kernel(skipped, n_msgs, scale, per, rows, stride, *refs):
    q, own, msgs = refs[0], refs[1], refs[2 : 2 + n_msgs]
    olds, outs = refs[2 + n_msgs : -3], refs[-3:]
    hd = own.shape[1]
    blocks = split(msgs, stride)
    part = document_part(own, blocks[: len(blocks) - skipped], rows, stride)
    eye = pick(rows, per)
    span = per * rows
    for b in range(q.shape[1] // hd // per):
        cut = slice(b * span, (b + 1) * span)
        qx = jnp.concatenate([heads_of(q, b, per, hd), eye], axis=1)
        state = tuple(ref[cut] for ref in olds) if olds else None
        for ref, x in zip(outs, attend(qx, part, scale * log2_e, state)):
            ref[cut] = x


def gradient_kernel(first_blocks, masks, scale, per, rows, stride, *refs):
    q, t = refs[:2]
    olds = refs[2:5]
    outs, grad = refs[-4:-1], refs[-1]
    msgs = refs[5:-4]
    own = msgs[0]
    hd = own.shape[1]
    crows = (stride - 2 * rows - 16) // 2
    me = lax.axis_index("ctx")
    two = scale * log2_e
    part = document_part(own, split(msgs, stride)[first_blocks:], rows, stride)
    every = [(ref, at + 2 * rows) for ref, at in split(msgs, stride)]
    cart_k = jnp.concatenate([ref[at : at + crows] for ref, at in every], axis=0)
    cart_v = jnp.concatenate([ref[at + crows : at + 2 * crows] for ref, at in every], axis=0)
    cart_vx = jnp.concatenate([cart_v, jnp.ones_like(cart_v)], axis=1)
    n_cart = cart_k.shape[0]
    eye = pick(rows, per)
    span = per * rows
    gk = jnp.zeros((n_cart, hd), f32)
    gv = jnp.zeros((n_cart, hd), f32)
    for b in range(q.shape[1] // hd // per):
        cut = slice(b * span, (b + 1) * span)
        qh = heads_of(q, b, per, hd)
        acc, total, top = attend(jnp.concatenate([qh, eye], axis=1), part, two, tuple(ref[cut] for ref in olds))
        for ref, x in zip(outs, (acc, total, top)):
            ref[cut] = x
        sc = nt(qh, cart_k) * two
        both = jnp.maximum(top, jnp.max(sc, axis=1, keepdims=True))
        wc = jnp.exp2(sc - wide(both, n_cart))
        keep = jnp.exp2(top - both)
        more = nn(wc.astype(bf16), cart_vx)
        inv = 1.0 / (total * keep + more[:, hd:])
        out = (acc * keep + more[:, :hd]) * inv
        d_out = out - heads_of(t, b, per, hd).astype(f32)
        delta = jnp.sum(d_out * out, axis=1, keepdims=True)
        d_out_b = d_out.astype(bf16)
        probs = wc * wide(inv, n_cart)
        ds = probs * (nt(d_out_b, cart_v) - delta)
        gk = gk + tn(ds.astype(bf16), qh)
        gv = gv + tn(probs.astype(bf16), d_out_b)
    whole = jnp.concatenate([gk * scale, gv], axis=1).astype(bf16)
    for j, mask in enumerate(masks):
        to = pl.multiple_of((me ^ mask) * crows, crows)
        grad[pl.ds(to, crows)] = whole[j * crows : (j + 1) * crows]


def summed(parts):
    parts = [x.astype(f32) for x in parts]
    if len(parts) == 2:
        return parts[0] + parts[1]
    own, one, two, both = parts
    return (own + both) + (one + two)


def square_kernel(*refs):
    total, squares = refs[-2:]
    g = summed([ref[...] for ref in refs[:-2]])
    total[...] = g
    squares[...] = jnp.broadcast_to(jnp.sum(g * g, keepdims=True), squares.shape)


def update(g, ma, m1, m2):
    one = beta_one * m1 + (1.0 - beta_one) * g
    two = beta_two * m2 + (1.0 - beta_two) * g * g
    return one, two, ma - learn_rate * one / (jnp.sqrt(two) + adam_eps)


def final_kernel(masks, chain, n_dp, scale, per, count, q, acc_in, total_in, top_in, g, sq_a, sq_b, st_near, st_far, *rest):
    rows, hd = q.shape[0], acc_in.shape[1]
    group = q.shape[1] // hd
    crows, width = rest[1].shape[0], rest[1].shape[2]
    me, my_dp = lax.axis_index("ctx"), lax.axis_index("dp")
    two = scale * log2_e
    out_hbm, small_hbm = rest[0], rest[1:4]
    out, small, cart, sems = rest[4], rest[5:8], rest[8], rest[9]
    copies = []

    def send(source, target):
        copies.append(pltpu.make_async_copy(source, target, sems.at[len(copies)]))
        copies[-1].start()

    mean = (sq_a[0:1, 0:1] + sq_b[0:1, 0:1]) * (1.0 / count)
    inv_rms = 1.0 / jnp.sqrt(mean + norm_eps)
    mine = g[pl.ds(pl.multiple_of(me * crows, crows), crows)]
    own = mine[:, 0:width]
    for d in range(1, n_dp):
        own = jnp.where(my_dp == d, mine[:, d * width : (d + 1) * width], own)
    one, sec, new = update(own * inv_rms, *(st_near[n * crows : (n + 1) * crows] for n in range(3)))
    for ref, target, x in zip(small, small_hbm, (new, one, sec)):
        ref[:, 0, :] = x
        send(ref, target)
    for r, mask in enumerate(masks):
        parts = [[], [], []]
        st = st_far if mask & chain[-1][1] else st_near
        for d in range(n_dp):
            at = (spot(chain[:-1], "ctx", mask) + spot(chain[:-1], "dp", my_dp ^ d)) * 3 * crows
            for n in range(3):
                parts[n].append(st[pl.ds(pl.multiple_of(at + n * crows, crows), crows)])
        ma_r, m1_r, m2_r = (jnp.concatenate(x, axis=1) for x in parts)
        rows_g = g[pl.ds(pl.multiple_of((me ^ mask) * crows, crows), crows)]
        _, _, new = update(rows_g * inv_rms, ma_r, m1_r, m2_r)
        cart[r * crows : (r + 1) * crows] = new.astype(bf16)
    cart_k = cart[:, :hd]
    cart_v = cart[:, hd:]
    cart_vx = jnp.concatenate([cart_v, jnp.ones_like(cart_v)], axis=1)
    span = per * rows
    for b in range(group // per):
        heads = range(b * per, (b + 1) * per)
        qh = jnp.concatenate([q[:, h * hd : (h + 1) * hd] for h in heads], axis=0)
        cut = slice(b * span, (b + 1) * span)
        top = top_in[cut]
        sc = nt(qh, cart_k) * two
        both = jnp.maximum(top, jnp.max(sc, axis=1, keepdims=True))
        wc = jnp.exp2(sc - wide(both, sc.shape[1])).astype(bf16)
        keep = jnp.exp2(top - both)
        more = nn(wc, cart_vx)
        res = ((acc_in[cut] * keep + more[:, :hd]) / (total_in[cut] * keep + more[:, hd:])).astype(bf16)
        for n, h in enumerate(heads):
            out[:, h * hd : (h + 1) * hd] = res[n * rows : (n + 1) * rows]
        columns = slice(b * per * hd, (b + 1) * per * hd)
        send(out.at[:, columns], out_hbm.at[:, columns])
    for copy in copies:
        copy.wait()


VMEM = pl.BlockSpec(memory_space=pltpu.VMEM)


def call(body, outs, n_in, scratch=(), limit=40, space=VMEM):
    return pl.pallas_call(
        body,
        out_shape=outs,
        in_specs=[VMEM] * n_in,
        out_specs=tuple(space for _ in outs),
        scratch_shapes=list(scratch),
        compiler_params=pltpu.CompilerParams(vmem_limit_bytes=limit * 2**20),
    )


def local(sizes, queries, targets, document_keys, document_values, doc_pos, cart_keys, cartridge_values, master, first_moment1, second_moment2):
    n_dp, n_ctx, n_head = sizes
    hd = document_keys.shape[2]
    rows = queries.shape[1]
    group = queries.shape[2] // hd
    crows = cart_keys.shape[0]
    scale = hd ** (-0.5)
    steps, dp_steps, head_steps = xor_steps(n_ctx), xor_steps(n_dp), xor_steps(n_head)
    sds = jax.ShapeDtypeStruct
    stride = 2 * rows + 2 * crows + 16
    masks = [0]
    for s in steps:
        masks += [m ^ s for m in masks]
    msg, st = pl.pallas_call(
        pack_kernel,
        out_shape=(sds((stride, hd), bf16), sds((3 * crows, master.shape[2]), f32)),
        in_specs=[pl.BlockSpec(memory_space=pltpu.HBM)] * 8,
        out_specs=(VMEM, VMEM),
        scratch_shapes=[pltpu.VMEM(doc_pos.shape, jnp.int32), pltpu.SemaphoreType.DMA((8,))],
        compiler_params=pltpu.CompilerParams(vmem_limit_bytes=8 * 2**20),
    )(
        *(
            pltpu.with_memory_space_constraint(x, pltpu.HBM)
            for x in (document_keys, document_values, doc_pos, cart_keys, cartridge_values, master, first_moment1, second_moment2)
        )
    )
    q, t = queries[0], targets[0]
    cart = n_ctx * crows
    shapes = (sds((rows * group, hd), f32),) * 3
    last = steps[-1]
    held, fresh, unsent, mirrored = [msg], [msg], [msg], []
    for s in steps[:-1]:
        older = held[: len(held) - len(fresh)]
        early = [swap(joined(older), "ctx", s, n_ctx)] if older else []
        newest = [swap(joined(fresh), "ctx", s, n_ctx)]
        mirrored.append(swap(joined(unsent + early), "ctx", last, n_ctx))
        fresh, unsent = early + newest, newest
        held = held + fresh
    mirrored.append(swap(joined(unsent), "ctx", last, n_ctx))
    msgs = held + mirrored
    tail = mirrored[-1].shape[0] // stride
    left = max(2, tail)
    q = pl.pallas_call(
        fetch_kernel,
        out_shape=sds(q.shape, q.dtype),
        in_specs=[pl.BlockSpec(memory_space=pltpu.HBM)],
        out_specs=VMEM,
        scratch_shapes=[pltpu.SemaphoreType.DMA],
        compiler_params=pltpu.CompilerParams(vmem_limit_bytes=8 * 2**20),
    )(pltpu.with_memory_space_constraint(q, pltpu.HBM))

    def document(some, skipped, state):
        body = functools.partial(chunk_kernel, skipped, len(some), scale, math.gcd(group, 4 if state else 2), rows, stride)
        return call(body, shapes, 2 + len(some) + len(state))(q, msg, *some, *state)

    state = document(held[:-1] + mirrored[:-2], 0, ())
    state = document(held[-1:] + mirrored[-2:-1], left - tail, state)
    chain = [("ctx", s) for s in steps]
    chain[1:1] = [("dp", s) for s in dp_steps]
    for n, (axis, s) in enumerate(chain):
        if n:
            st = lax.optimization_barrier(jnp.concatenate([st, more], axis=0))
        more = swap(st, axis, s, {"ctx": n_ctx, "dp": n_dp}[axis])
    body = functools.partial(gradient_kernel, n_ctx - left, masks, scale, math.gcd(group, 16), rows, stride)
    *state, grad = call(body, shapes + (sds((cart, 2 * hd), bf16),), 5 + len(msgs))(q, t, *state, *msgs)
    bits = steps + [s * n_ctx for s in dp_steps]
    rounds = [bits[n : n + 2] for n in range(0, len(bits), 2)]
    for n, pair in enumerate(rounds):
        ways = pair + [sum(pair)] if len(pair) == 2 else pair
        others = [swap(grad, ("dp", "ctx"), m, n_dp * n_ctx) for m in ways]
        if n + 1 < len(rounds):
            grad = summed([grad] + others).astype(bf16)
    total, squares = call(square_kernel, (sds((cart, 2 * hd), f32), sds((8, hd), f32)), 1 + len(others))(grad, *others)
    mine = squares
    theirs = jnp.zeros_like(squares)
    for n, s in enumerate(head_steps):
        if n:
            mine = mine + theirs
        theirs = swap(mine, "head", s, n_head)
    count = master.size * n_dp * n_ctx * n_head
    new_out, new_master, new_m1, new_m2 = call(
        functools.partial(final_kernel, masks, chain, n_dp, scale, math.gcd(group, 8), count),
        (sds((rows, group * hd), bf16),) + (sds(master.shape, f32),) * 3,
        9,
        [pltpu.VMEM((rows, group * hd), bf16)]
        + [pltpu.VMEM(master.shape, f32)] * 3
        + [pltpu.VMEM((cart, 2 * hd), bf16), pltpu.SemaphoreType.DMA((3 + group,))],
        space=pl.BlockSpec(memory_space=pltpu.HBM),
    )(q, *state, total, mine, theirs, st, more)
    return (new_out[None], new_master, new_m1, new_m2)


def solution(mesh):
    in_specs = (
        P("dp", "ctx", "head"),
        P("dp", "ctx", "head"),
        P("dp", "ctx", "head"),
        P("dp", "ctx", "head"),
        P("dp", "ctx"),
        P("ctx", "head"),
        P("ctx", "head"),
        P("ctx", "head", "dp"),
        P("ctx", "head", "dp"),
        P("ctx", "head", "dp"),
    )
    out_specs = (
        P("dp", "ctx", "head"),
        P("ctx", "head", "dp"),
        P("ctx", "head", "dp"),
        P("ctx", "head", "dp"),
    )
    sizes = (mesh.shape["dp"], mesh.shape["ctx"], mesh.shape["head"])

    def step(*args):
        return local(sizes, *args)

    return jax.shard_map(step, mesh=mesh, in_specs=in_specs, out_specs=out_specs, check_vma=False)
```
